32 devices in a mesh: slab: 2 (over y), sec: 8 (over z, x), tile: 2 (over core).
Axes of the slice: x: 2, y: 2, z: 4, core: 2. Of those that a mesh axis runs over, the one named last changes fastest.
Arguments:
- image: bfloat16 [16, 128, 4096], P(('slab', 'sec'), 'tile'), parts along dimension 0, may hold values from -6 to 6
- keyframe: int32 [16], P(('slab', 'sec')), parts along dimension 0, may hold values from 0 to 7, as said below
- offsets: int32 [16, 64], P(('slab', 'sec')), parts along dimension 0, may hold values from -16 to 16
Outputs:
- warped: bfloat16 [16, 128, 4096], P(('slab', 'sec'), 'tile'), parts along dimension 0
- field: float32 [16, 2, 2, 64], P(('slab', 'sec'), None, 'tile'), parts along dimension 0
- pyramid: float32 [16, 16, 512], P(('slab', 'sec'), 'tile'), parts along dimension 0
The draws below stay inside these ranges and needn't reach their ends.
There are 2 independent parts, one for each index of `slab`. The reference program is written for one: setup_inputs(seed, part) draws one part's arguments, and reference() takes and returns one part's arrays. A program takes and returns all parts, laid end to end along the dimension named above; each array names one. Nothing has to cross between parts.
Inputs may be any that keep to these rules, and one draw needn't show every extreme that they name: Sections 0, 3 and 7 are keyframes and section 4 is not; keyframe[s] is the largest keyframe index at or before s, and a keyframe is its own keyframe.
All inputs are finite; a program needn't handle non-finite values.
Results may differ from the reference program's by a relative error of at most 0.0033.
Values may be sent and summed in bfloat16 or wider, within the bound.
A program may use at most 64 MiB of HBM per device.

```python
import jax
import jax.numpy as jnp
from jax import lax

W = 4096
PATCH = 64
KCOEF = 8
OFFMAX = 16
WIN = 8
SECTIONS = 8
ROWS = 128


def draw_keyframe(key, part):
    marks = jax.random.randint(jax.random.fold_in(key, 71), (SECTIONS,), 0, 2) == 0
    index = jnp.arange(SECTIONS, dtype=jnp.int32)
    middle = SECTIONS // 2
    marks = marks | (index == 0) | (index == SECTIONS - 1) | (index == middle - 1)
    marks = marks & (index != middle)
    return lax.cummax(jnp.where(marks, index, 0), axis=0).astype(jnp.int32)


def plant(array, stream_key, smallest, largest):
    index_at = [jax.random.randint(jax.random.fold_in(stream_key, axis), (), 0, length) for axis, length in enumerate(array.shape)]
    longest = array.shape.index(max(array.shape))
    neighbour = index_at[:longest] + [(index_at[longest] + 1) % array.shape[longest]] + index_at[longest + 1:]
    return array.at[tuple(index_at)].set(smallest).at[tuple(neighbour)].set(largest)


def block_levels(stream_key, shape, cuts, low, high):
    factor_of = 1.0
    for axis_at, shards_of in cuts:
        steps = jax.random.uniform(jax.random.fold_in(jax.random.fold_in(stream_key, 6), axis_at), (shards_of,), jnp.float32, low / len(cuts), high / len(cuts))
        factor_of = factor_of * jnp.repeat(jnp.exp(steps), shape[axis_at] // shards_of).reshape((-1,) + (1,) * (len(shape) - 1 - axis_at))
    return factor_of


def normal_values(key, dims, deviation, bound, cuts=(), held_as=jnp.bfloat16):
    values = deviation * jax.random.normal(key, dims, jnp.float32)
    if cuts:
        values = values * block_levels(key, dims, cuts, -0.22, 0.18)
    return jnp.clip(values, -bound, bound).astype(held_as)


def setup_inputs(seed: int = 0, part: int = 0) -> dict:
    streams_of = jax.random.split(jax.random.key(seed), 4)
    own_keys = jax.random.split(jax.random.fold_in(streams_of[3], part), 4)
    image = normal_values(own_keys[0], (SECTIONS, ROWS, W), 1.0, 6.0, ((0, 8), (1, 2)))
    keyframe = draw_keyframe(jax.random.fold_in(jax.random.fold_in(streams_of[3], part), 71), part)
    offsets = plant(jax.random.randint(own_keys[2], (SECTIONS, W // PATCH), 0 - OFFMAX, OFFMAX + 1), jax.random.fold_in(own_keys[2], 1), 0 - OFFMAX, OFFMAX).astype(jnp.int32)
    return {"image": image, "keyframe": keyframe, "offsets": offsets}


HIGH = lax.Precision.HIGHEST
REG = 4.0

def cosine_table():
    index = jnp.arange(PATCH, dtype=jnp.float32)
    order = jnp.arange(KCOEF, dtype=jnp.float32)
    table = jnp.sqrt(2.0 / PATCH) * jnp.cos(jnp.pi * (index[None, :] + 0.5) * order[:, None] / PATCH)
    scale = jnp.where(order == 0, jnp.sqrt(0.5), 1.0)
    return (table * scale[:, None]).astype(jnp.float32)

def describe(field, table):
    rows, cols = field.shape
    first = jnp.einsum('rtj,bj->rtb', field.reshape(rows, cols // PATCH, PATCH), table, precision=HIGH)
    first = first.reshape(rows // PATCH, PATCH, cols // PATCH * KCOEF)
    second = jnp.einsum('pic,ai->pac', first, table, precision=HIGH)
    return second.reshape(rows // PATCH * KCOEF, cols // PATCH * KCOEF)

def patch_sums(values):
    rows, cols = values.shape
    return values.reshape(rows // KCOEF, KCOEF, cols // KCOEF, KCOEF).sum(axis=(1, 3))

def displacement(desc, d_col, d_row, refer):
    diff = refer.astype(jnp.float32) - desc.astype(jnp.float32)
    gxx = patch_sums(d_col * d_col) + REG
    gxy = patch_sums(d_col * d_row)
    gyy = patch_sums(d_row * d_row) + REG
    b_col = patch_sums(d_col * diff)
    b_row = patch_sums(d_row * diff)
    det = gxx * gyy - gxy * gxy
    return ((gyy * b_col - gxy * b_row) / det, (gxx * b_row - gxy * b_col) / det)

def taps(shift):
    return (-shift * (shift - 1.0) * (shift - 2.0) / 6.0, (shift + 1.0) * (shift - 1.0) * (shift - 2.0) / 2.0, -(shift + 1.0) * shift * (shift - 2.0) / 2.0, (shift + 1.0) * shift * (shift - 1.0) / 6.0)

def warp(extended, u_col, u_row, offs):
    rows = extended.shape[0] - 4
    cols = extended.shape[1]
    prow, pcol = (rows // PATCH, cols // PATCH)
    vert = jnp.zeros((prow, PATCH, pcol, PATCH), jnp.float32)
    for k, weight in enumerate(taps(u_row)):
        part = extended[1 + k:1 + k + rows].reshape(prow, PATCH, pcol, PATCH)
        vert = vert + weight[:, None, :, None] * part
    padded = jnp.pad(vert, ((0, 0), (0, 0), (1, 1), (0, 0)))
    window = jnp.concatenate([padded[:, :, 0:pcol], padded[:, :, 1:pcol + 1], padded[:, :, 2:pcol + 2]], axis=-1)
    widx = jnp.arange(3 * PATCH, dtype=jnp.int32)[None, None, :, None]
    jidx = jnp.arange(PATCH, dtype=jnp.int32)[None, None, None, :]
    base = jidx + PATCH + offs.astype(jnp.int32)[None, :, None, None]
    matrix = jnp.zeros((prow, pcol, 3 * PATCH, PATCH), jnp.float32)
    for k, weight in enumerate(taps(u_col)):
        matrix = matrix + weight[:, :, None, None] * (widx == base + (k - 1)).astype(jnp.float32)
    out = jnp.einsum('pitw,ptwj->pitj', window, matrix, precision=HIGH)
    return out.reshape(rows, cols)

def reference(image, keyframe, offsets):
    table = cosine_table()

    def first_pass(section):
        ext = jnp.pad(section.astype(jnp.float32), ((2, 2), (1, 1)))
        center = ext[2:-2, 1:-1]
        g_col = (ext[2:-2, 2:] - ext[2:-2, :-2]) * 0.5
        g_row = (ext[3:-1, 1:-1] - ext[1:-3, 1:-1]) * 0.5
        return (describe(center, table).astype(jnp.bfloat16), describe(g_col, table), describe(g_row, table))
    desc, d_col, d_row = lax.map(first_pass, image)
    keyref = jnp.take(desc, keyframe, axis=0)
    predref = jnp.concatenate([jnp.zeros_like(desc[:1]), desc[:-1]], axis=0)

    def second_pass(items):
        section, own, dc, dr, kref, pref, offs = items
        kc, kr = displacement(own, dc, dr, kref)
        pc, pr = displacement(own, dc, dr, pref)
        u_col = 0.5 * (kc + pc)
        u_row = 0.5 * (kr + pr)
        extended = jnp.pad(section.astype(jnp.float32), ((2, 2), (0, 0)))
        out = warp(extended, u_col, u_row, offs)
        rows, cols = out.shape
        block = out.reshape(rows // 8, 8, cols // 8, 8).sum(axis=(1, 3))
        return (out.astype(jnp.bfloat16), jnp.stack([u_col, u_row]), block)
    warped, field, block = lax.map(second_pass, (image, desc, d_col, d_row, keyref, predref, offsets))
    total = jnp.cumsum(block, axis=0)
    earlier = jnp.concatenate([jnp.zeros((WIN,) + block.shape[1:], jnp.float32), total[:-WIN]], axis=0)
    pyramid = (total - earlier) / 512.0
    return (warped, field, pyramid)
```

```python
import functools

import jax
import jax.numpy as jnp
import ml_dtypes
import numpy as np
from jax import lax
from jax.experimental import pallas as pl
from jax.experimental.pallas import tpu as pltpu
from jax.sharding import PartitionSpec as P

PATCH = 64
KCOEF = 8
WIN = 8
REG = 4.0
BOX = 8
LANES = 128
PAD = 16
CHUNK = 8
FAR_AT = 9
MESH = pl.DeviceIdType.MESH
F32 = jnp.float32
BF16 = jnp.bfloat16


def np_split(value, terms):
    parts = []
    rest = np.asarray(value, np.float64)
    for _ in range(terms):
        part = rest.astype(np.float32).astype(ml_dtypes.bfloat16)
        parts.append(part)
        rest = rest - part.astype(np.float64)
    return parts


def cosines():
    index = np.arange(PATCH, dtype=np.float64)
    order = np.arange(KCOEF, dtype=np.float64)
    table = np.sqrt(2.0 / PATCH) * np.cos(np.pi * (index[None, :] + 0.5) * order[:, None] / PATCH)
    table = table * np.where(order == 0, np.sqrt(0.5), 1.0)[:, None]
    return table.astype(np.float32).astype(np.float64)


def row_tables(rows):
    table = cosines()
    ext = rows + 2 * PAD
    first = np.concatenate(np_split(table, 2), axis=0)
    slope = np.zeros((KCOEF, ext))
    slope[:, PAD + 1 : PAD + 1 + rows] += 0.5 * table
    slope[:, PAD - 1 : PAD - 1 + rows] -= 0.5 * table
    second = np_split(slope, 2)
    for k in range(-1, 3):
        sums = np.zeros((rows // BOX, ext))
        for r in range(rows):
            sums[r // BOX, PAD + r + k] = 1.0
        second.append(sums.astype(ml_dtypes.bfloat16))
    return first, np.concatenate(second, axis=0)


def column_tables():
    table = cosines()
    slope = np.zeros((PATCH, KCOEF))
    slope[1:] += 0.5 * table.T[:-1]
    slope[:-1] -= 0.5 * table.T[1:]
    times = (1, LANES // KCOEF)
    pieces = []
    for both in (np_split(np.concatenate([np.tile(table.T, times), np.tile(slope, times)], axis=1), 2)):
        pieces.append(both)
    ends = np.zeros((16, LANES))
    ends[0] = np.tile(-0.5 * table[:, 0], LANES // KCOEF)
    ends[1] = np.tile(0.5 * table[:, PATCH - 1], LANES // KCOEF)
    return np.stack(pieces), np.stack(np_split(ends, 2))


def across_tables():
    shift = np.zeros((2 * LANES, 4, LANES))
    for k in range(-1, 3):
        for c in range(LANES):
            shift[(0 if c < PATCH else LANES) + (c + k) % LANES, k + 1, c] = 1.0
    slots = LANES // BOX
    pooled = shift.reshape(2 * LANES, 4, slots, BOX).sum(axis=3)
    pooled = np.tile(pooled, (1, 1, LANES // slots)).reshape(2 * LANES, 4 * LANES)
    outer = shift[:, (0, 3)].reshape(2 * LANES, 2 * LANES)
    return outer.astype(ml_dtypes.bfloat16), pooled.astype(ml_dtypes.bfloat16)


def gather_table(coefs):
    found = np.zeros((coefs, LANES))
    for i in range(coefs):
        found[i, i // KCOEF :: coefs // KCOEF] = 1.0
    return found.astype(ml_dtypes.bfloat16)


def split(value, terms):
    parts = []
    for _ in range(terms):
        part = value.astype(BF16)
        parts.append(part)
        value = value - part.astype(F32)
    return parts


def dot(a, b):
    return jnp.dot(a, b, preferred_element_type=F32)


def to_groups(value, width):
    count = value.shape[1] // width
    return jnp.concatenate([value[:, g * width : (g + 1) * width] for g in range(count)], axis=0)


def from_groups(value, count):
    rows = value.shape[0] // count
    return jnp.concatenate([value[g * rows : (g + 1) * rows] for g in range(count)], axis=1)


def taps(shift):
    return (
        -shift * (shift - 1.0) * (shift - 2.0) * (1.0 / 6.0),
        (shift + 1.0) * (shift - 1.0) * (shift - 2.0) * 0.5,
        -(shift + 1.0) * shift * (shift - 2.0) * 0.5,
        (shift + 1.0) * shift * (shift - 1.0) * (1.0 / 6.0),
    )


def stacked(value, times):
    return value if times == 1 else jnp.concatenate([value] * times, axis=0)


def kernel(
    n, tiles, kf_hbm, off_hbm, first_hbm, second_hbm, piece_hbm, ends_hbm, outer_hbm, pooled_hbm, compact_hbm, boxes_hbm, x_hbm,
    obuf, field_ref, pyr_ref,
    kf_ref, off_ref, first_ref, second_ref, piece_ref, ends_ref, outer_ref, pooled_ref, compact, boxes_ref,
    xext, xtall, expand, colw, comm, sums_ref, vsum, lhs_s, vert, lhs, weights, brecv, bsend, block_ref,
    load_sem, table_sem, halo_ssem, halo_rsem, ssem, rsem, bssem, brsem, far_sem,
):
    me = lax.axis_index("sec")
    mt = lax.axis_index("tile")
    _, rows, cols = obuf.shape
    group = LANES // KCOEF * PATCH
    groups = cols // group
    blocks = cols // LANES
    sums = rows // BOX

    barrier = pltpu.get_barrier_semaphore()
    load = pltpu.make_async_copy(x_hbm.at[0], xext.at[pl.ds(PAD, rows)], load_sem)
    fetches = [
        pltpu.make_async_copy(source, target, table_sem.at[i])
        for i, (source, target) in enumerate((
            (piece_hbm, piece_ref), (ends_hbm, ends_ref), (first_hbm, first_ref), (second_hbm, second_ref),
            (kf_hbm, kf_ref), (off_hbm, off_ref), (compact_hbm, compact), (pooled_hbm, pooled_ref),
            (boxes_hbm, boxes_ref), (outer_hbm, outer_ref),
        ))
    ]
    reach = min(WIN, n) - 1
    middle = n // 2 - 1
    start = jnp.where(me >= n - 1, n - 1, jnp.where(me >= middle, middle, 0))
    stop = jnp.where(me < middle, middle, n - 1)
    first = jnp.maximum(jnp.minimum(start, me - 1), 0)
    last = jnp.minimum(jnp.maximum(stop - 1, me + 1), n - 1)
    far_first = jnp.minimum(jnp.maximum(me - reach, 0), first)
    far_last = jnp.maximum(jnp.minimum(me + reach, n - 1), last)

    def greet(q, carry):
        pl.semaphore_signal(barrier, inc=1, device_id={"sec": q}, device_id_type=MESH)
        return carry

    lax.fori_loop(first, me, greet, 0)
    lax.fori_loop(last + 1, far_last + 1, greet, 0)

    @pl.when(mt > 0)
    def _():
        pl.semaphore_signal(barrier, inc=1, device_id={"tile": mt - 1}, device_id_type=MESH)

    @pl.when(mt < tiles - 1)
    def _():
        pl.semaphore_signal(barrier, inc=1, device_id={"tile": mt + 1}, device_id_type=MESH)

    for fetch in fetches[:3]:
        fetch.start()
    load.start()
    for fetch in fetches[3:7]:
        fetch.start()

    for edge in (0, blocks + 1):
        at = slice(edge * LANES, (edge + 1) * LANES)
        vert[:, at] = jnp.zeros((rows, LANES), BF16)
        vsum[:, at] = jnp.zeros((sums, LANES), F32)

    fetches[0].wait()
    fetches[1].wait()
    own = lax.broadcasted_iota(jnp.int32, (PATCH, LANES), 1) // KCOEF
    row_of = lax.broadcasted_iota(jnp.int32, (PATCH, LANES), 0)

    def build_columns(p, carry):
        at = pl.ds(pl.multiple_of(p * PATCH, PATCH), PATCH)
        for term in range(2):
            piece = piece_ref[term].astype(F32)
            ends = ends_ref[term].astype(F32)
            colw[term, at, 0:LANES] = jnp.where(own == p, piece[:, :LANES], 0.0).astype(BF16)
            slope = jnp.where(own == p, piece[:, LANES:], 0.0)
            slope = jnp.where((own == p + 1) & (row_of == PATCH - 1), ends[0:1], slope)
            slope = jnp.where((own == p - 1) & (row_of == 0), ends[1:2], slope)
            colw[term, at, LANES : 2 * LANES] = slope.astype(BF16)
        return carry

    lax.fori_loop(0, group // PATCH, build_columns, 0)
    side = lax.broadcasted_iota(jnp.int32, (LANES, LANES), 1) // KCOEF
    deep = lax.broadcasted_iota(jnp.int32, (LANES, LANES), 0)
    for term in range(2):
        ends = ends_ref[term].astype(F32)
        tail = jnp.where((side == LANES // KCOEF - 1) & (deep == 0), ends[1:2], 0.0)
        tail = jnp.where((side == 0) & (deep == LANES - 1), ends[0:1], tail)
        colw[term, group : group + LANES, 0:LANES] = jnp.zeros((LANES, LANES), BF16)
        colw[term, group : group + LANES, LANES : 2 * LANES] = tail.astype(BF16)

    fetches[2].wait()
    load.wait()
    for fetch in fetches[7:]:
        fetch.start()

    part = dot(first_ref[...], xext[PAD : PAD + rows, :])
    t_full = part[0:KCOEF] + part[KCOEF : 2 * KCOEF]
    lane8 = lax.broadcasted_iota(jnp.int32, (KCOEF, LANES), 1)
    edges = []
    for g in range(groups):
        edge = jnp.zeros((KCOEF, LANES), F32)
        if g > 0:
            edge = jnp.where(lane8 == LANES - 1, t_full[:, g * group - LANES : g * group], edge)
        if g < groups - 1:
            edge = jnp.where(lane8 == 0, t_full[:, (g + 1) * group : (g + 1) * group + LANES], edge)
        edges.append(edge)
    parts = split(jnp.concatenate([to_groups(t_full, group), jnp.concatenate(edges, axis=0)], axis=1), 2)
    size = groups * KCOEF
    wide = dot(jnp.concatenate(parts, axis=0), colw[0])
    wide = wide[:size] + wide[size:] + dot(parts[0], colw[1])
    desc = from_groups(wide[:, :LANES], groups).astype(BF16)
    dx = from_groups(wide[:, LANES:], groups)
    comm[me] = desc

    pl.semaphore_wait(
        barrier,
        (last - me) + (first - far_first) + (mt > 0).astype(jnp.int32) + (mt < tiles - 1).astype(jnp.int32),
    )

    def desc_copy(target):
        return pltpu.make_async_remote_copy(
            src_ref=comm.at[me], dst_ref=comm.at[me], send_sem=ssem.at[target], recv_sem=rsem.at[me],
            device_id={"sec": target}, device_id_type=MESH,
        )

    def send_desc(target, carry):
        desc_copy(target).start()
        return carry

    def admit(q, carry):
        pl.semaphore_signal(far_sem, inc=1, device_id={"sec": q}, device_id_type=MESH)
        return carry

    lax.fori_loop(me + 1, last + 1, send_desc, 0)
    lax.fori_loop(far_first, first, admit, 0)

    to_next = pltpu.make_async_remote_copy(
        src_ref=xext.at[pl.ds(rows, PAD)], dst_ref=xext.at[pl.ds(0, PAD)],
        send_sem=halo_ssem.at[0], recv_sem=halo_rsem.at[0],
        device_id={"tile": jnp.minimum(mt + 1, tiles - 1)}, device_id_type=MESH,
    )
    to_last = pltpu.make_async_remote_copy(
        src_ref=xext.at[pl.ds(PAD, PAD)], dst_ref=xext.at[pl.ds(PAD + rows, PAD)],
        send_sem=halo_ssem.at[1], recv_sem=halo_rsem.at[1],
        device_id={"tile": jnp.maximum(mt - 1, 0)}, device_id_type=MESH,
    )

    @pl.when(mt < tiles - 1)
    def _():
        to_next.start()

    @pl.when(mt > 0)
    def _():
        to_last.start()

    def build_expand(v, carry):
        at = pl.ds(pl.multiple_of(v * LANES, LANES), LANES)
        patch = 2 * v + lax.broadcasted_iota(jnp.int32, (LANES, LANES), 1) // PATCH
        expand[:, at] = jnp.where(deep % (LANES // 2) == patch, 1.0, 0.0).astype(BF16)
        return carry

    lax.fori_loop(0, blocks, build_expand, 0)
    @pl.when(mt == 0)
    def _():
        xext[0:PAD, :] = jnp.zeros((PAD, cols), BF16)

    @pl.when(mt == tiles - 1)
    def _():
        xext[PAD + rows : 2 * PAD + rows, :] = jnp.zeros((PAD, cols), BF16)

    fetches[3].wait()

    @pl.when(mt < tiles - 1)
    def _():
        to_last.wait_recv()

    @pl.when(mt > 0)
    def _():
        to_next.wait_recv()

    part = dot(second_ref[...], xext[...])
    t_full = part[0:KCOEF] + part[KCOEF : 2 * KCOEF]
    for j in range(4):
        begin = 2 * KCOEF + j * sums
        sums_ref[j] = part[begin : begin + sums]
    for v in range(blocks):
        at = slice(v * LANES, (v + 1) * LANES)
        xtall[v] = xext[:, at].astype(F32)
    parts = split(to_groups(t_full, group), 2)
    wide = dot(jnp.concatenate(parts, axis=0), colw[0, 0:group, 0:LANES])
    dy = from_groups(wide[:size] + wide[size:] + dot(parts[0], colw[1, 0:group, 0:LANES]), groups)

    def row_total(value):
        for step in (4, 2, 1):
            value = value + pltpu.roll(value, step, 0)
        return value

    fetches[6].wait()

    def narrow(values):
        left = jnp.concatenate(values, axis=0)
        size = left.shape[0]
        wide = dot(jnp.concatenate(split(left, 3), axis=0), compact[...])
        total = wide[:size] + (wide[size : 2 * size] + wide[2 * size :])
        step = size // len(values)
        return [row_total(total[i * step : (i + 1) * step]) for i in range(len(values))]

    gxx, gxy, gyy = narrow([dx * dx, dx * dy, dy * dy])
    gxx = gxx + REG
    gyy = gyy + REG
    scale = 1.0 / (gxx * gyy - gxy * gxy)

    fetches[4].wait()
    fetches[5].wait()

    def wait_desc(q, carry):
        pltpu.make_async_remote_copy(
            src_ref=comm.at[q], dst_ref=comm.at[q], send_sem=ssem.at[q], recv_sem=rsem.at[q],
            device_id={"sec": q}, device_id_type=MESH,
        ).wait_recv()
        return carry

    lax.fori_loop(first, me, wait_desc, 0)

    keyref = comm[kf_ref[0]].astype(F32)
    predref = jnp.where(me > 0, comm[jnp.maximum(me - 1, 0)].astype(F32), 0.0)
    diff = 0.5 * (keyref + predref) - desc.astype(F32)
    bx, by = narrow([dx * diff, dy * diff])
    ux = (gyy * bx - gxy * by) * scale
    uy = (gxx * by - gxy * bx) * scale
    field_ref[0, 0] = ux[0:1, 0 : cols // PATCH]
    field_ref[0, 1] = uy[0:1, 0 : cols // PATCH]

    which = lax.broadcasted_iota(jnp.int32, (KCOEF, LANES), 0)
    picked = None
    for k, weight in enumerate(taps(ux) + taps(uy)):
        picked = weight if picked is None else jnp.where(which == k, weight, picked)
    coarse = picked.astype(BF16)
    fine = (picked - coarse.astype(F32)).astype(BF16)
    halves = jnp.where(lane8 < LANES // 2, coarse.astype(F32), fine.astype(F32)).astype(BF16)
    weights[...] = dot(halves, expand[...])

    def combine(terms, first, at):
        times = terms[0].shape[0] // KCOEF
        total = None
        for k, term in enumerate(terms):
            factor = jnp.broadcast_to(weights[first + k : first + k + 1, at], (KCOEF, term.shape[1]))
            term = stacked(factor, times) * term
            total = term if total is None else total + term
        return total

    for v in range(blocks):
        at = slice(v * LANES, (v + 1) * LANES)
        vsum[:, LANES + v * LANES : 2 * LANES + v * LANES] = combine([sums_ref[k, :, at] for k in range(4)], 4, at)

    def turned(ref, v, count):
        left, center, right = (ref[0:count, pl.ds(pl.multiple_of((v + i) * LANES, LANES), LANES)] for i in range(3))
        lane = lax.broadcasted_iota(jnp.int32, (count, LANES), 1)
        even = jnp.where(lane >= 96, left, center)
        odd = jnp.where(lane < 32, right, center)
        return (
            pltpu.roll(even, (LANES - off_ref[0, 2 * v]) & (LANES - 1), 1),
            pltpu.roll(odd, (LANES - off_ref[0, 2 * v + 1]) & (LANES - 1), 1),
        )

    for v in range(0, blocks, 2):
        pairs = [turned(vsum, v + i, sums) for i in range(2)]
        for i in range(2):
            lhs_s[v * sums : (v + 2) * sums, i * LANES : (i + 1) * LANES] = jnp.concatenate(
                [pair[i] for pair in pairs], axis=0
            ).astype(BF16)
    fetches[7].wait()
    fetches[8].wait()
    small = dot(halves, boxes_ref[...])
    slots = LANES // BOX
    per = LANES // slots
    slot = lane8 // slots
    for m in range(blocks // per):
        wide = dot(lhs_s[m * per * sums : (m + 1) * per * sums, :], pooled_ref[...])
        picked = None
        for i in range(per):
            piece = wide[i * sums : (i + 1) * sums]
            piece = [piece[:, j * LANES : (j + 1) * LANES] for j in range(4)]
            picked = piece if i == 0 else [jnp.where(slot == i, new, old) for new, old in zip(piece, picked)]
        at = slice(m * LANES, (m + 1) * LANES)
        total = None
        for k in range(4):
            term = jnp.broadcast_to(small[k : k + 1, at], (sums, LANES)) * picked[k]
            total = term if total is None else total + term
        block_ref[:, at] = total
        bsend[:, at] = total.astype(BF16)

    def block_copy(target):
        return pltpu.make_async_remote_copy(
            src_ref=bsend, dst_ref=brecv.at[target - me - 1], send_sem=bssem.at[target - me - 1],
            recv_sem=brsem.at[target - me - 1], device_id={"sec": target}, device_id_type=MESH,
        )

    def send_block(target, carry):
        block_copy(target).start()
        return carry

    lax.fori_loop(me + 1, jnp.minimum(last, me + reach) + 1, send_block, 0)

    def send_far():
        @pl.when(far_last > last)
        def _():
            pl.semaphore_wait(far_sem, far_last - last)

        lax.fori_loop(last + 1, far_last + 1, send_block, 0)

    fetches[9].wait()

    def vertical(v):
        at = slice(v * LANES, (v + 1) * LANES)
        total = combine([xtall[v, PAD + k : PAD + k + rows] for k in range(-1, 3)], 4, at)
        vert[:, (v + 1) * LANES : (v + 2) * LANES] = total.astype(BF16)

    def turn(v):
        even, odd = turned(vert, v, rows)
        lhs[v * rows : (v + 1) * rows, 0:LANES] = even
        lhs[v * rows : (v + 1) * rows, LANES : 2 * LANES] = odd

    lane64 = lax.broadcasted_iota(jnp.int32, (rows, LANES), 1)

    def across(g):
        wide = dot(lhs[g * CHUNK * rows : (g + 1) * CHUNK * rows, :], outer_ref[...])
        for i in range(CHUNK):
            v = g * CHUNK + i
            at = slice(v * LANES, (v + 1) * LANES)
            even = lhs[v * rows : (v + 1) * rows, 0:LANES]
            odd = lhs[v * rows : (v + 1) * rows, LANES : 2 * LANES]
            center = jnp.where(lane64 < PATCH, even, odd)
            after = pltpu.roll(jnp.where(((lane64 - 1) & (LANES - 1)) < PATCH, even, odd), LANES - 1, 1)
            piece = wide[i * rows : (i + 1) * rows]
            terms = [piece[:, :LANES], center.astype(F32), after.astype(F32), piece[:, LANES:]]
            obuf[0, :, at] = combine(terms, 0, at).astype(BF16)

    steps = blocks // CHUNK
    vertical(0)
    for step in range(steps + 2):
        if step == FAR_AT:
            send_far()
        if 0 <= step - 2:
            across(step - 2)
        if 0 <= step - 1 < steps:
            for i in range(CHUNK):
                turn((step - 1) * CHUNK + i)
        if step < steps:
            for i in range(CHUNK):
                if step * CHUNK + i + 1 < blocks:
                    vertical(step * CHUNK + i + 1)

    if FAR_AT > steps + 1:
        send_far()
    pyr_ref[0] = block_ref[...]
    for d in range(1, reach + 1):
        @pl.when(me >= d)
        def _():
            pltpu.make_async_remote_copy(
                src_ref=bsend, dst_ref=brecv.at[d - 1], send_sem=bssem.at[d - 1], recv_sem=brsem.at[d - 1],
                device_id={"sec": jnp.maximum(me - d, 0)}, device_id_type=MESH,
            ).wait_recv()
            pyr_ref[0] = pyr_ref[0] + brecv[d - 1].astype(F32)
    pyr_ref[0] = pyr_ref[0] * (1.0 / (BOX * BOX * WIN))

    def sent_desc(target, carry):
        desc_copy(target).wait_send()
        return carry

    def sent_block(target, carry):
        block_copy(target).wait_send()
        return carry

    lax.fori_loop(me + 1, last + 1, sent_desc, 0)
    lax.fori_loop(me + 1, jnp.minimum(me + reach, n - 1) + 1, sent_block, 0)

    @pl.when(mt < tiles - 1)
    def _():
        to_next.wait_send()

    @pl.when(mt > 0)
    def _():
        to_last.wait_send()


def write_out(a, b, c, a_out, b_out, c_out, sem):
    copies = [
        pltpu.make_async_copy(source, target, sem.at[i])
        for i, (source, target) in enumerate(((a, a_out), (b, b_out), (c, c_out)))
    ]
    for copy in copies:
        copy.start()
    for copy in copies:
        copy.wait()


def body(n, tiles, image, keyframe, offsets):
    _, rows, cols = image.shape
    first, second = row_tables(rows)
    piece, ends = column_tables()
    outer, pooled = across_tables()
    ext = rows + 2 * PAD
    sums = rows // BOX
    coefs = cols // PATCH * KCOEF
    group = LANES // KCOEF * PATCH
    compact = gather_table(coefs)
    constants = (first, second, piece, ends, outer, pooled, compact, np.ascontiguousarray(compact.T))
    vmem = pl.BlockSpec(memory_space=pltpu.VMEM)
    hbm = pl.BlockSpec(memory_space=pltpu.HBM)
    dma = pltpu.SemaphoreType.DMA
    results = pl.pallas_call(
        functools.partial(kernel, n, tiles),
        out_shape=(
            pltpu.VMEM(image.shape, BF16),
            pltpu.VMEM((1, 2, 1, cols // PATCH), F32),
            pltpu.VMEM((1, sums, cols // BOX), F32),
        ),
        in_specs=[hbm] * (3 + len(constants)),
        out_specs=(vmem, vmem, vmem),
        scratch_shapes=[
            pltpu.SMEM((1,), jnp.int32),
            pltpu.SMEM((1, cols // PATCH), jnp.int32),
            *[pltpu.VMEM(value.shape, BF16) for value in constants],
            pltpu.VMEM((ext, cols), BF16),
            pltpu.VMEM((cols // LANES, ext, LANES), F32),
            pltpu.VMEM((LANES, cols), BF16),
            pltpu.VMEM((2, group + LANES, 2 * LANES), BF16),
            pltpu.VMEM((n, KCOEF, coefs), BF16),
            pltpu.VMEM((4, sums, cols), F32),
            pltpu.VMEM((sums, cols + 2 * LANES), F32),
            pltpu.VMEM((cols // LANES * sums, 2 * LANES), BF16),
            pltpu.VMEM((rows, cols + 2 * LANES), BF16),
            pltpu.VMEM((cols // LANES * rows, 2 * LANES), BF16),
            pltpu.VMEM((KCOEF, cols), F32),
            pltpu.VMEM((WIN - 1, sums, cols // BOX), BF16),
            pltpu.VMEM((sums, cols // BOX), BF16),
            pltpu.VMEM((sums, cols // BOX), F32),
            dma,
            dma((10,)),
            dma((2,)),
            dma((2,)),
            dma((n,)),
            dma((n,)),
            dma((WIN - 1,)),
            dma((WIN - 1,)),
            pltpu.SemaphoreType.REGULAR,
        ],
        compiler_params=pltpu.CompilerParams(collective_id=0, has_side_effects=True),
    )(keyframe, offsets, *[jnp.asarray(value) for value in constants], image)
    return pl.pallas_call(
        write_out,
        out_shape=tuple(jax.ShapeDtypeStruct(r.shape, r.dtype) for r in results),
        in_specs=[vmem] * 3,
        out_specs=(hbm,) * 3,
        scratch_shapes=[dma((3,))],
    )(*[pltpu.with_memory_space_constraint(r, pltpu.VMEM) for r in results])


def solution(mesh):
    return jax.shard_map(
        functools.partial(body, mesh.shape["sec"], mesh.shape["tile"]),
        mesh=mesh,
        in_specs=(P(("slab", "sec"), "tile", None), P(("slab", "sec")), P(("slab", "sec"), None)),
        out_specs=(
            P(("slab", "sec"), "tile", None),
            P(("slab", "sec"), None, "tile", None),
            P(("slab", "sec"), "tile", None),
        ),
        check_vma=False,
    )
```

```python
import functools

import jax
import jax.numpy as jnp
import ml_dtypes
import numpy as np
from jax import lax
from jax.experimental import pallas as pl
from jax.experimental.pallas import tpu as pltpu
from jax.sharding import PartitionSpec as P

PATCH = 64
KCOEF = 8
WIN = 8
REG = 4.0
BOX = 8
LANES = 128
PAD = 16
CHUNK = 8
EARLY = 1
SOME_AT = 2
MESH = pl.DeviceIdType.MESH
F32 = jnp.float32
BF16 = jnp.bfloat16


def np_split(value, terms):
    parts = []
    rest = np.asarray(value, np.float64)
    for _ in range(terms):
        part = rest.astype(np.float32).astype(ml_dtypes.bfloat16)
        parts.append(part)
        rest = rest - part.astype(np.float64)
    return parts


def cosines():
    index = np.arange(PATCH, dtype=np.float64)
    order = np.arange(KCOEF, dtype=np.float64)
    table = np.sqrt(2.0 / PATCH) * np.cos(np.pi * (index[None, :] + 0.5) * order[:, None] / PATCH)
    table = table * np.where(order == 0, np.sqrt(0.5), 1.0)[:, None]
    return table.astype(np.float32).astype(np.float64)


def row_tables(rows):
    table = cosines()
    ext = rows + 2 * PAD
    first = np.concatenate(np_split(table, 2), axis=0)
    slope = np.zeros((KCOEF, ext))
    slope[:, PAD + 1 : PAD + 1 + rows] += 0.5 * table
    slope[:, PAD - 1 : PAD - 1 + rows] -= 0.5 * table
    second = np_split(slope, 2)
    for k in range(-1, 3):
        sums = np.zeros((rows // BOX, ext))
        for r in range(rows):
            sums[r // BOX, PAD + r + k] = 1.0
        second.append(sums.astype(ml_dtypes.bfloat16))
    return first, np.concatenate(second, axis=0)


def column_tables():
    table = cosines()
    slope = np.zeros((PATCH, KCOEF))
    slope[1:] += 0.5 * table.T[:-1]
    slope[:-1] -= 0.5 * table.T[1:]
    times = (1, LANES // KCOEF)
    pieces = []
    for both in (np_split(np.concatenate([np.tile(table.T, times), np.tile(slope, times)], axis=1), 2)):
        pieces.append(both)
    ends = np.zeros((16, LANES))
    ends[0] = np.tile(-0.5 * table[:, 0], LANES // KCOEF)
    ends[1] = np.tile(0.5 * table[:, PATCH - 1], LANES // KCOEF)
    return np.stack(pieces), np.stack(np_split(ends, 2))


def across_tables():
    shift = np.zeros((2 * LANES, 4, LANES))
    for k in range(-1, 3):
        for c in range(LANES):
            shift[(0 if c < PATCH else LANES) + (c + k) % LANES, k + 1, c] = 1.0
    slots = LANES // BOX
    pooled = shift.reshape(2 * LANES, 4, slots, BOX).sum(axis=3)
    pooled = np.tile(pooled, (1, 1, LANES // slots)).reshape(2 * LANES, 4 * LANES)
    outer = shift[:, (0, 3)].reshape(2 * LANES, 2 * LANES)
    return outer.astype(ml_dtypes.bfloat16), pooled.astype(ml_dtypes.bfloat16)


def gather_table(coefs):
    found = np.zeros((coefs, LANES))
    for i in range(coefs):
        found[i, i // KCOEF :: coefs // KCOEF] = 1.0
    return found.astype(ml_dtypes.bfloat16)


def split(value, terms):
    parts = []
    for _ in range(terms):
        part = value.astype(BF16)
        parts.append(part)
        value = value - part.astype(F32)
    return parts


def dot(a, b):
    return jnp.dot(a, b, preferred_element_type=F32)


def to_groups(value, width):
    count = value.shape[1] // width
    return jnp.concatenate([value[:, g * width : (g + 1) * width] for g in range(count)], axis=0)


def from_groups(value, count):
    rows = value.shape[0] // count
    return jnp.concatenate([value[g * rows : (g + 1) * rows] for g in range(count)], axis=1)


def taps(shift):
    return (
        -shift * (shift - 1.0) * (shift - 2.0) * (1.0 / 6.0),
        (shift + 1.0) * (shift - 1.0) * (shift - 2.0) * 0.5,
        -(shift + 1.0) * shift * (shift - 2.0) * 0.5,
        (shift + 1.0) * shift * (shift - 1.0) * (1.0 / 6.0),
    )


def stacked(value, times):
    return value if times == 1 else jnp.concatenate([value] * times, axis=0)


def kernel(
    n, tiles, kf_hbm, off_hbm, first_hbm, second_hbm, piece_hbm, ends_hbm, outer_hbm, pooled_hbm, compact_hbm, x_hbm,
    obuf, field_ref, pyr_ref,
    kf_ref, off_ref, first_ref, second_ref, piece_ref, ends_ref, outer_ref, pooled_ref, compact,
    xext, xtall, colw, comm, sums_ref, vsum, lhs_s, vert, lhs, weights, brecv, bsend, block_ref,
    load_sem, table_sem, halo_ssem, halo_rsem, ssem, rsem, bssem, brsem, far_sem,
):
    me = lax.axis_index("sec")
    mt = lax.axis_index("tile")
    _, rows, cols = obuf.shape
    group = LANES // KCOEF * PATCH
    groups = cols // group
    blocks = cols // LANES
    sums = rows // BOX

    barrier = pltpu.get_barrier_semaphore()
    load = pltpu.make_async_copy(x_hbm.at[0], xext.at[pl.ds(PAD, rows)], load_sem)
    fetches = [
        pltpu.make_async_copy(source, target, table_sem.at[i])
        for i, (source, target) in enumerate((
            (piece_hbm, piece_ref), (ends_hbm, ends_ref), (first_hbm, first_ref), (second_hbm, second_ref),
            (kf_hbm, kf_ref), (off_hbm, off_ref), (compact_hbm, compact), (pooled_hbm, pooled_ref),
            (outer_hbm, outer_ref),
        ))
    ]
    reach = min(WIN, n) - 1
    middle = n // 2 - 1
    start = jnp.where(me >= n - 1, n - 1, jnp.where(me >= middle, middle, 0))
    stop = jnp.where(me < middle, middle, n - 1)
    first = jnp.maximum(jnp.minimum(start, me - 1), 0)
    last = jnp.minimum(jnp.maximum(stop - 1, me + 1), n - 1)
    far_first = jnp.minimum(jnp.maximum(me - reach, 0), first)
    far_last = jnp.maximum(jnp.minimum(me + reach, n - 1), last)

    def greet(q, carry):
        pl.semaphore_signal(barrier, inc=1, device_id={"sec": q}, device_id_type=MESH)
        return carry

    lax.fori_loop(first, me, greet, 0)
    lax.fori_loop(last + 1, far_last + 1, greet, 0)

    @pl.when(mt > 0)
    def _():
        pl.semaphore_signal(barrier, inc=1, device_id={"tile": mt - 1}, device_id_type=MESH)

    @pl.when(mt < tiles - 1)
    def _():
        pl.semaphore_signal(barrier, inc=1, device_id={"tile": mt + 1}, device_id_type=MESH)

    for fetch in fetches[:3]:
        fetch.start()
    load.start()
    for fetch in fetches[3:7]:
        fetch.start()

    for edge in (0, blocks + 1):
        at = slice(edge * LANES, (edge + 1) * LANES)
        vert[:, at] = jnp.zeros((rows, LANES), BF16)
        vsum[:, at] = jnp.zeros((sums, LANES), F32)

    fetches[0].wait()
    fetches[1].wait()
    own = lax.broadcasted_iota(jnp.int32, (PATCH, LANES), 1) // KCOEF
    row_of = lax.broadcasted_iota(jnp.int32, (PATCH, LANES), 0)

    def build_columns(p, carry):
        at = pl.ds(pl.multiple_of(p * PATCH, PATCH), PATCH)
        for term in range(2):
            piece = piece_ref[term].astype(F32)
            ends = ends_ref[term].astype(F32)
            colw[term, at, 0:LANES] = jnp.where(own == p, piece[:, :LANES], 0.0).astype(BF16)
            slope = jnp.where(own == p, piece[:, LANES:], 0.0)
            slope = jnp.where((own == p + 1) & (row_of == PATCH - 1), ends[0:1], slope)
            slope = jnp.where((own == p - 1) & (row_of == 0), ends[1:2], slope)
            colw[term, at, LANES : 2 * LANES] = slope.astype(BF16)
        return carry

    lax.fori_loop(0, group // PATCH, build_columns, 0)
    side = lax.broadcasted_iota(jnp.int32, (LANES, LANES), 1) // KCOEF
    deep = lax.broadcasted_iota(jnp.int32, (LANES, LANES), 0)
    for term in range(2):
        ends = ends_ref[term].astype(F32)
        tail = jnp.where((side == LANES // KCOEF - 1) & (deep == 0), ends[1:2], 0.0)
        tail = jnp.where((side == 0) & (deep == LANES - 1), ends[0:1], tail)
        colw[term, group : group + LANES, 0:LANES] = jnp.zeros((LANES, LANES), BF16)
        colw[term, group : group + LANES, LANES : 2 * LANES] = tail.astype(BF16)

    def admit(q, carry):
        pl.semaphore_signal(far_sem.at[me - q - 1], inc=1, device_id={"sec": q}, device_id_type=MESH)
        return carry

    def meet():
        pl.semaphore_wait(
            barrier,
            (last - me) + (first - far_first) + (mt > 0).astype(jnp.int32) + (mt < tiles - 1).astype(jnp.int32),
        )
        lax.fori_loop(far_first, first, admit, 0)

    pl.when(last == me)(meet)
    fetches[2].wait()
    load.wait()
    for fetch in fetches[7:]:
        fetch.start()

    part = dot(first_ref[...], xext[PAD : PAD + rows, :])
    t_full = part[0:KCOEF] + part[KCOEF : 2 * KCOEF]
    lane8 = lax.broadcasted_iota(jnp.int32, (KCOEF, LANES), 1)
    edges = []
    for g in range(groups):
        edge = jnp.zeros((KCOEF, LANES), F32)
        if g > 0:
            edge = jnp.where(lane8 == LANES - 1, t_full[:, g * group - LANES : g * group], edge)
        if g < groups - 1:
            edge = jnp.where(lane8 == 0, t_full[:, (g + 1) * group : (g + 1) * group + LANES], edge)
        edges.append(edge)
    parts = split(jnp.concatenate([to_groups(t_full, group), jnp.concatenate(edges, axis=0)], axis=1), 2)
    size = groups * KCOEF
    wide = dot(jnp.concatenate(parts, axis=0), colw[0])
    wide = wide[:size] + wide[size:] + dot(parts[0], colw[1])
    desc = from_groups(wide[:, :LANES], groups).astype(BF16)
    dx = from_groups(wide[:, LANES:], groups)
    comm[me] = desc

    pl.when(last > me)(meet)

    def desc_copy(target):
        return pltpu.make_async_remote_copy(
            src_ref=comm.at[me], dst_ref=comm.at[me], send_sem=ssem.at[target], recv_sem=rsem.at[me],
            device_id={"sec": target}, device_id_type=MESH,
        )

    def send_desc(target, carry):
        desc_copy(target).start()
        return carry

    lax.fori_loop(me + 1, last + 1, send_desc, 0)

    to_next = pltpu.make_async_remote_copy(
        src_ref=xext.at[pl.ds(rows, PAD)], dst_ref=xext.at[pl.ds(0, PAD)],
        send_sem=halo_ssem.at[0], recv_sem=halo_rsem.at[0],
        device_id={"tile": jnp.minimum(mt + 1, tiles - 1)}, device_id_type=MESH,
    )
    to_last = pltpu.make_async_remote_copy(
        src_ref=xext.at[pl.ds(PAD, PAD)], dst_ref=xext.at[pl.ds(PAD + rows, PAD)],
        send_sem=halo_ssem.at[1], recv_sem=halo_rsem.at[1],
        device_id={"tile": jnp.maximum(mt - 1, 0)}, device_id_type=MESH,
    )

    @pl.when(mt < tiles - 1)
    def _():
        to_next.start()

    @pl.when(mt > 0)
    def _():
        to_last.start()

    @pl.when(mt == 0)
    def _():
        xext[0:PAD, :] = jnp.zeros((PAD, cols), BF16)

    @pl.when(mt == tiles - 1)
    def _():
        xext[PAD + rows : 2 * PAD + rows, :] = jnp.zeros((PAD, cols), BF16)

    fetches[3].wait()

    @pl.when(mt < tiles - 1)
    def _():
        to_last.wait_recv()

    @pl.when(mt > 0)
    def _():
        to_next.wait_recv()

    part = dot(second_ref[...], xext[...])
    t_full = part[0:KCOEF] + part[KCOEF : 2 * KCOEF]
    for j in range(4):
        begin = 2 * KCOEF + j * sums
        sums_ref[j] = part[begin : begin + sums]
    for v in range(blocks):
        at = slice(v * LANES, (v + 1) * LANES)
        xtall[v] = xext[:, at].astype(F32)
    parts = split(to_groups(t_full, group), 2)
    wide = dot(jnp.concatenate(parts, axis=0), colw[0, 0:group, 0:LANES])
    dy = from_groups(wide[:size] + wide[size:] + dot(parts[0], colw[1, 0:group, 0:LANES]), groups)

    def row_total(value):
        for step in (4, 2, 1):
            value = value + pltpu.roll(value, step, 0)
        return value

    fetches[6].wait()

    def narrow(values):
        left = jnp.concatenate(values, axis=0)
        size = left.shape[0]
        wide = dot(jnp.concatenate(split(left, 3), axis=0), compact[...])
        total = wide[:size] + (wide[size : 2 * size] + wide[2 * size :])
        step = size // len(values)
        return [row_total(total[i * step : (i + 1) * step]) for i in range(len(values))]

    gxx, gxy, gyy = narrow([dx * dx, dx * dy, dy * dy])
    gxx = gxx + REG
    gyy = gyy + REG
    scale = 1.0 / (gxx * gyy - gxy * gxy)

    fetches[4].wait()
    fetches[5].wait()

    def wait_desc(q, carry):
        pltpu.make_async_remote_copy(
            src_ref=comm.at[q], dst_ref=comm.at[q], send_sem=ssem.at[q], recv_sem=rsem.at[q],
            device_id={"sec": q}, device_id_type=MESH,
        ).wait_recv()
        return carry

    lax.fori_loop(first, me, wait_desc, 0)

    keyref = comm[kf_ref[0]].astype(F32)
    predref = jnp.where(me > 0, comm[jnp.maximum(me - 1, 0)].astype(F32), 0.0)
    diff = 0.5 * (keyref + predref) - desc.astype(F32)
    bx, by = narrow([dx * diff, dy * diff])
    ux = (gyy * bx - gxy * by) * scale
    uy = (gxx * by - gxy * bx) * scale
    field_ref[0, 0] = ux[0:1, 0 : cols // PATCH]
    field_ref[0, 1] = uy[0:1, 0 : cols // PATCH]

    which = lax.broadcasted_iota(jnp.int32, (KCOEF, LANES), 0)
    picked = None
    for k, weight in enumerate(taps(ux) + taps(uy)):
        picked = weight if picked is None else jnp.where(which == k, weight, picked)
    picked_taps = picked
    half = jnp.where(lane8 < PATCH, 0, 1)
    for v in range(blocks):
        weights[:, v * LANES : (v + 1) * LANES] = jnp.take_along_axis(picked, half + 2 * v, axis=1)

    def combine(terms, first, at):
        times = terms[0].shape[0] // KCOEF
        total = None
        for k, term in enumerate(terms):
            factor = jnp.broadcast_to(weights[first + k : first + k + 1, at], (KCOEF, term.shape[1]))
            term = stacked(factor, times) * term
            total = term if total is None else total + term
        return total

    for v in range(blocks):
        at = slice(v * LANES, (v + 1) * LANES)
        vsum[:, LANES + v * LANES : 2 * LANES + v * LANES] = combine([sums_ref[k, :, at] for k in range(4)], 4, at)

    def turned(ref, v, count):
        left, center, right = (ref[0:count, pl.ds(pl.multiple_of((v + i) * LANES, LANES), LANES)] for i in range(3))
        lane = lax.broadcasted_iota(jnp.int32, (count, LANES), 1)
        even = jnp.where(lane >= 96, left, center)
        odd = jnp.where(lane < 32, right, center)
        return (
            pltpu.roll(even, (LANES - off_ref[0, 2 * v]) & (LANES - 1), 1),
            pltpu.roll(odd, (LANES - off_ref[0, 2 * v + 1]) & (LANES - 1), 1),
        )

    for v in range(0, blocks, 2):
        pairs = [turned(vsum, v + i, sums) for i in range(2)]
        for i in range(2):
            lhs_s[v * sums : (v + 2) * sums, i * LANES : (i + 1) * LANES] = jnp.concatenate(
                [pair[i] for pair in pairs], axis=0
            ).astype(BF16)
    fetches[7].wait()
    slots = LANES // BOX
    per = LANES // slots
    slot = lane8 // slots
    for m in range(blocks // per):
        wide = dot(lhs_s[m * per * sums : (m + 1) * per * sums, :], pooled_ref[...])
        picked = None
        for i in range(per):
            piece = wide[i * sums : (i + 1) * sums]
            piece = [piece[:, j * LANES : (j + 1) * LANES] for j in range(4)]
            picked = piece if i == 0 else [jnp.where(slot == i, new, old) for new, old in zip(piece, picked)]
        at = slice(m * LANES, (m + 1) * LANES)
        small = jnp.take_along_axis(picked_taps, lane8 // BOX + m * slots, axis=1)
        total = None
        for k in range(4):
            term = jnp.broadcast_to(small[k : k + 1], (sums, LANES)) * picked[k]
            total = term if total is None else total + term
        block_ref[:, at] = total
        bsend[:, at] = total.astype(BF16)

    def block_copy(target):
        return pltpu.make_async_remote_copy(
            src_ref=bsend, dst_ref=brecv.at[target - me - 1], send_sem=bssem.at[target - me - 1],
            recv_sem=brsem.at[target - me - 1], device_id={"sec": target}, device_id_type=MESH,
        )

    def send_block(target, carry):
        block_copy(target).start()
        return carry

    lax.fori_loop(me + 1, jnp.minimum(last, me + reach) + 1, send_block, 0)

    def send_far_block(target, carry):
        pl.semaphore_wait(far_sem.at[target - me - 1], 1)
        return send_block(target, carry)

    near = last + 1 + lax.rem(last + 1 + me, 2)
    away = last + 1 + lax.rem(last + me, 2)
    n_near = jnp.maximum(far_last - near + 2, 0) // 2
    n_away = jnp.maximum(far_last - away + 2, 0) // 2

    def send_far(begin):
        lax.fori_loop(begin, n_near, lambda i, carry: send_far_block(near + 2 * i, carry), 0)
        lax.fori_loop(0, n_away, lambda i, carry: send_far_block(away + 2 * i, carry), 0)

    @pl.when(me >= EARLY)
    def _():
        send_far(0)

    fetches[8].wait()

    def vertical(v):
        at = slice(v * LANES, (v + 1) * LANES)
        total = combine([xtall[v, PAD + k : PAD + k + rows] for k in range(-1, 3)], 4, at)
        vert[:, (v + 1) * LANES : (v + 2) * LANES] = total.astype(BF16)

    def turn(v):
        even, odd = turned(vert, v, rows)
        lhs[v * rows : (v + 1) * rows, 0:LANES] = even
        lhs[v * rows : (v + 1) * rows, LANES : 2 * LANES] = odd

    lane64 = lax.broadcasted_iota(jnp.int32, (rows, LANES), 1)

    def across(g):
        wide = dot(lhs[g * CHUNK * rows : (g + 1) * CHUNK * rows, :], outer_ref[...])
        for i in range(CHUNK):
            v = g * CHUNK + i
            at = slice(v * LANES, (v + 1) * LANES)
            even = lhs[v * rows : (v + 1) * rows, 0:LANES]
            odd = lhs[v * rows : (v + 1) * rows, LANES : 2 * LANES]
            center = jnp.where(lane64 < PATCH, even, odd)
            after = pltpu.roll(jnp.where(((lane64 - 1) & (LANES - 1)) < PATCH, even, odd), LANES - 1, 1)
            piece = wide[i * rows : (i + 1) * rows]
            terms = [piece[:, :LANES], center.astype(F32), after.astype(F32), piece[:, LANES:]]
            obuf[0, :, at] = combine(terms, 0, at).astype(BF16)

    steps = blocks // CHUNK
    vertical(0)
    for step in range(steps + 2):
        if step == SOME_AT:
            @pl.when((me < EARLY) & (n_near > 0))
            def _():
                send_far_block(near, 0)

        if 0 <= step - 2:
            across(step - 2)
        if 0 <= step - 1 < steps:
            for i in range(CHUNK):
                turn((step - 1) * CHUNK + i)
        if step < steps:
            for i in range(CHUNK):
                if step * CHUNK + i + 1 < blocks:
                    vertical(step * CHUNK + i + 1)

    @pl.when(me < EARLY)
    def _():
        send_far(jnp.minimum(n_near, 1))

    pyr_ref[0] = block_ref[...]
    for d in range(reach, 0, -1):
        @pl.when(me >= d)
        def _():
            pltpu.make_async_remote_copy(
                src_ref=bsend, dst_ref=brecv.at[d - 1], send_sem=bssem.at[d - 1], recv_sem=brsem.at[d - 1],
                device_id={"sec": jnp.maximum(me - d, 0)}, device_id_type=MESH,
            ).wait_recv()
            pyr_ref[0] = pyr_ref[0] + brecv[d - 1].astype(F32)
    pyr_ref[0] = pyr_ref[0] * (1.0 / (BOX * BOX * WIN))

    def sent_desc(target, carry):
        desc_copy(target).wait_send()
        return carry

    def sent_block(target, carry):
        block_copy(target).wait_send()
        return carry

    lax.fori_loop(me + 1, last + 1, sent_desc, 0)
    lax.fori_loop(me + 1, jnp.minimum(me + reach, n - 1) + 1, sent_block, 0)

    @pl.when(mt < tiles - 1)
    def _():
        to_next.wait_send()

    @pl.when(mt > 0)
    def _():
        to_last.wait_send()


def write_out(a, b, c, a_out, b_out, c_out, sem):
    copies = [
        pltpu.make_async_copy(source, target, sem.at[i])
        for i, (source, target) in enumerate(((a, a_out), (b, b_out), (c, c_out)))
    ]
    for copy in copies:
        copy.start()
    for copy in copies:
        copy.wait()


def body(n, tiles, image, keyframe, offsets):
    _, rows, cols = image.shape
    first, second = row_tables(rows)
    piece, ends = column_tables()
    outer, pooled = across_tables()
    ext = rows + 2 * PAD
    sums = rows // BOX
    coefs = cols // PATCH * KCOEF
    group = LANES // KCOEF * PATCH
    compact = gather_table(coefs)
    constants = (first, second, piece, ends, outer, pooled, compact)
    vmem = pl.BlockSpec(memory_space=pltpu.VMEM)
    hbm = pl.BlockSpec(memory_space=pltpu.HBM)
    dma = pltpu.SemaphoreType.DMA
    results = pl.pallas_call(
        functools.partial(kernel, n, tiles),
        out_shape=(
            pltpu.VMEM(image.shape, BF16),
            pltpu.VMEM((1, 2, 1, cols // PATCH), F32),
            pltpu.VMEM((1, sums, cols // BOX), F32),
        ),
        in_specs=[hbm] * (3 + len(constants)),
        out_specs=(vmem, vmem, vmem),
        scratch_shapes=[
            pltpu.SMEM((1,), jnp.int32),
            pltpu.SMEM((1, cols // PATCH), jnp.int32),
            *[pltpu.VMEM(value.shape, BF16) for value in constants],
            pltpu.VMEM((ext, cols), BF16),
            pltpu.VMEM((cols // LANES, ext, LANES), F32),
            pltpu.VMEM((2, group + LANES, 2 * LANES), BF16),
            pltpu.VMEM((n, KCOEF, coefs), BF16),
            pltpu.VMEM((4, sums, cols), F32),
            pltpu.VMEM((sums, cols + 2 * LANES), F32),
            pltpu.VMEM((cols // LANES * sums, 2 * LANES), BF16),
            pltpu.VMEM((rows, cols + 2 * LANES), BF16),
            pltpu.VMEM((cols // LANES * rows, 2 * LANES), BF16),
            pltpu.VMEM((KCOEF, cols), F32),
            pltpu.VMEM((WIN - 1, sums, cols // BOX), BF16),
            pltpu.VMEM((sums, cols // BOX), BF16),
            pltpu.VMEM((sums, cols // BOX), F32),
            dma,
            dma((9,)),
            dma((2,)),
            dma((2,)),
            dma((n,)),
            dma((n,)),
            dma((WIN - 1,)),
            dma((WIN - 1,)),
            pltpu.SemaphoreType.REGULAR((WIN - 1,)),
        ],
        compiler_params=pltpu.CompilerParams(collective_id=0, has_side_effects=True),
    )(keyframe, offsets, *[jnp.asarray(value) for value in constants], image)
    return pl.pallas_call(
        write_out,
        out_shape=tuple(jax.ShapeDtypeStruct(r.shape, r.dtype) for r in results),
        in_specs=[vmem] * 3,
        out_specs=(hbm,) * 3,
        scratch_shapes=[dma((3,))],
    )(*[pltpu.with_memory_space_constraint(r, pltpu.VMEM) for r in results])


def solution(mesh):
    return jax.shard_map(
        functools.partial(body, mesh.shape["sec"], mesh.shape["tile"]),
        mesh=mesh,
        in_specs=(P(("slab", "sec"), "tile", None), P(("slab", "sec")), P(("slab", "sec"), None)),
        out_specs=(
            P(("slab", "sec"), "tile", None),
            P(("slab", "sec"), None, "tile", None),
            P(("slab", "sec"), "tile", None),
        ),
        check_vma=False,
    )
```

```python
import functools

import jax
import jax.numpy as jnp
import ml_dtypes
import numpy as np
from jax import lax
from jax.experimental import pallas as pl
from jax.experimental.pallas import tpu as pltpu
from jax.sharding import PartitionSpec as P

PATCH = 64
KCOEF = 8
WIN = 8
REG = 4.0
BOX = 8
LANES = 128
PAD = 16
CHUNK = 8
MESH = pl.DeviceIdType.MESH
F32 = jnp.float32
BF16 = jnp.bfloat16


def np_split(value, terms):
    parts = []
    rest = np.asarray(value, np.float64)
    for _ in range(terms):
        part = rest.astype(np.float32).astype(ml_dtypes.bfloat16)
        parts.append(part)
        rest = rest - part.astype(np.float64)
    return parts


def cosines():
    index = np.arange(PATCH, dtype=np.float64)
    order = np.arange(KCOEF, dtype=np.float64)
    table = np.sqrt(2.0 / PATCH) * np.cos(np.pi * (index[None, :] + 0.5) * order[:, None] / PATCH)
    table = table * np.where(order == 0, np.sqrt(0.5), 1.0)[:, None]
    return table.astype(np.float32).astype(np.float64)


def row_tables(rows):
    table = cosines()
    ext = rows + 2 * PAD
    first = np.concatenate(np_split(table, 2), axis=0)
    slope = np.zeros((KCOEF, ext))
    slope[:, PAD + 1 : PAD + 1 + rows] += 0.5 * table
    slope[:, PAD - 1 : PAD - 1 + rows] -= 0.5 * table
    second = np_split(slope, 2)
    for k in range(-1, 3):
        sums = np.zeros((rows // BOX, ext))
        for r in range(rows):
            sums[r // BOX, PAD + r + k] = 1.0
        second.append(sums.astype(ml_dtypes.bfloat16))
    return first, np.concatenate(second, axis=0)


def column_tables():
    table = cosines()
    slope = np.zeros((PATCH, KCOEF))
    slope[1:] += 0.5 * table.T[:-1]
    slope[:-1] -= 0.5 * table.T[1:]
    times = (1, LANES // KCOEF)
    pieces = []
    for both in (np_split(np.concatenate([np.tile(table.T, times), np.tile(slope, times)], axis=1), 2)):
        pieces.append(both)
    ends = np.zeros((16, LANES))
    ends[0] = np.tile(-0.5 * table[:, 0], LANES // KCOEF)
    ends[1] = np.tile(0.5 * table[:, PATCH - 1], LANES // KCOEF)
    return np.stack(pieces), np.stack(np_split(ends, 2))


def across_tables():
    shift = np.zeros((2 * LANES, 4, LANES))
    for k in range(-1, 3):
        for c in range(LANES):
            shift[(0 if c < PATCH else LANES) + (c + k) % LANES, k + 1, c] = 1.0
    slots = LANES // BOX
    pooled = shift.reshape(2 * LANES, 4, slots, BOX).sum(axis=3)
    pooled = np.tile(pooled, (1, 1, LANES // slots)).reshape(2 * LANES, 4 * LANES)
    outer = shift[:, (0, 3)].reshape(2 * LANES, 2 * LANES)
    return outer.astype(ml_dtypes.bfloat16), pooled.astype(ml_dtypes.bfloat16)


def gather_table(coefs):
    found = np.zeros((coefs, LANES))
    for i in range(coefs):
        found[i, i // KCOEF :: coefs // KCOEF] = 1.0
    return found.astype(ml_dtypes.bfloat16)


def split(value, terms):
    parts = []
    for _ in range(terms):
        part = value.astype(BF16)
        parts.append(part)
        value = value - part.astype(F32)
    return parts


def dot(a, b):
    return jnp.dot(a, b, preferred_element_type=F32)


def to_groups(value, width):
    count = value.shape[1] // width
    return jnp.concatenate([value[:, g * width : (g + 1) * width] for g in range(count)], axis=0)


def from_groups(value, count):
    rows = value.shape[0] // count
    return jnp.concatenate([value[g * rows : (g + 1) * rows] for g in range(count)], axis=1)


def taps(shift):
    return (
        -shift * (shift - 1.0) * (shift - 2.0) * (1.0 / 6.0),
        (shift + 1.0) * (shift - 1.0) * (shift - 2.0) * 0.5,
        -(shift + 1.0) * shift * (shift - 2.0) * 0.5,
        (shift + 1.0) * shift * (shift - 1.0) * (1.0 / 6.0),
    )


def stacked(value, times):
    return value if times == 1 else jnp.concatenate([value] * times, axis=0)


def kernel(
    n, tiles, kf_hbm, off_hbm, first_hbm, second_hbm, piece_hbm, ends_hbm, outer_hbm, pooled_hbm, compact_hbm, x_hbm,
    obuf, field_ref, pyr_ref,
    kf_ref, off_ref, first_ref, second_ref, piece_ref, ends_ref, outer_ref, pooled_ref, compact,
    xext, xtall, colw, comm, sums_ref, vsum, lhs_s, vert, lhs, weights, brecv, bsend, block_ref,
    load_sem, table_sem, halo_ssem, halo_rsem, ssem, rsem, bssem, brsem, near_ok, far_ok,
):
    me = lax.axis_index("sec")
    mt = lax.axis_index("tile")
    _, rows, cols = obuf.shape
    group = LANES // KCOEF * PATCH
    groups = cols // group
    blocks = cols // LANES
    sums = rows // BOX

    barrier = pltpu.get_barrier_semaphore()
    load = pltpu.make_async_copy(x_hbm.at[0], xext.at[pl.ds(PAD, rows)], load_sem)
    fetches = [
        pltpu.make_async_copy(source, target, table_sem.at[i])
        for i, (source, target) in enumerate((
            (piece_hbm, piece_ref), (ends_hbm, ends_ref), (first_hbm, first_ref), (second_hbm, second_ref),
            (kf_hbm, kf_ref), (off_hbm, off_ref), (compact_hbm, compact), (pooled_hbm, pooled_ref),
            (outer_hbm, outer_ref),
        ))
    ]
    reach = min(WIN, n) - 1
    middle = n // 2 - 1
    start = jnp.where(me >= n - 1, n - 1, jnp.where(me >= middle, middle, 0))
    stop = jnp.where(me < middle, middle, n - 1)
    first = jnp.maximum(jnp.minimum(start, me - 1), 0)
    last = jnp.minimum(jnp.maximum(stop - 1, me + 1), n - 1)
    near_first = first
    near_last = last
    far_first = jnp.minimum(jnp.maximum(me - reach, 0), near_first)
    far_last = jnp.maximum(jnp.minimum(me + reach, n - 1), near_last)

    def greet(side, q, carry):
        pl.semaphore_signal(barrier, inc=1, device_id={"sec": q, "tile": side}, device_id_type=MESH)
        return carry

    lax.fori_loop(near_first, me, functools.partial(greet, 0), 0)
    lax.fori_loop(far_first, near_first, functools.partial(greet, tiles - 1), 0)

    @pl.when(mt > 0)
    def _():
        pl.semaphore_signal(barrier, inc=1, device_id={"tile": 0}, device_id_type=MESH)

    for fetch in fetches[:3]:
        fetch.start()
    load.start()
    for fetch in fetches[3:7]:
        fetch.start()

    for edge in (0, blocks + 1):
        at = slice(edge * LANES, (edge + 1) * LANES)
        vert[:, at] = jnp.zeros((rows, LANES), BF16)
        vsum[:, at] = jnp.zeros((sums, LANES), F32)

    fetches[0].wait()
    fetches[1].wait()
    own = lax.broadcasted_iota(jnp.int32, (PATCH, LANES), 1) // KCOEF
    row_of = lax.broadcasted_iota(jnp.int32, (PATCH, LANES), 0)

    def build_columns(p, carry):
        at = pl.ds(pl.multiple_of(p * PATCH, PATCH), PATCH)
        for term in range(2):
            piece = piece_ref[term].astype(F32)
            ends = ends_ref[term].astype(F32)
            colw[term, at, 0:LANES] = jnp.where(own == p, piece[:, :LANES], 0.0).astype(BF16)
            slope = jnp.where(own == p, piece[:, LANES:], 0.0)
            slope = jnp.where((own == p + 1) & (row_of == PATCH - 1), ends[0:1], slope)
            slope = jnp.where((own == p - 1) & (row_of == 0), ends[1:2], slope)
            colw[term, at, LANES : 2 * LANES] = slope.astype(BF16)
        return carry

    lax.fori_loop(0, group // PATCH, build_columns, 0)
    side = lax.broadcasted_iota(jnp.int32, (LANES, LANES), 1) // KCOEF
    deep = lax.broadcasted_iota(jnp.int32, (LANES, LANES), 0)
    for term in range(2):
        ends = ends_ref[term].astype(F32)
        tail = jnp.where((side == LANES // KCOEF - 1) & (deep == 0), ends[1:2], 0.0)
        tail = jnp.where((side == 0) & (deep == LANES - 1), ends[0:1], tail)
        colw[term, group : group + LANES, 0:LANES] = jnp.zeros((LANES, LANES), BF16)
        colw[term, group : group + LANES, LANES : 2 * LANES] = tail.astype(BF16)

    fetches[2].wait()
    load.wait()
    for fetch in fetches[7:]:
        fetch.start()

    part = dot(first_ref[...], xext[PAD : PAD + rows, :])
    t_full = part[0:KCOEF] + part[KCOEF : 2 * KCOEF]
    lane8 = lax.broadcasted_iota(jnp.int32, (KCOEF, LANES), 1)
    edges = []
    for g in range(groups):
        edge = jnp.zeros((KCOEF, LANES), F32)
        if g > 0:
            edge = jnp.where(lane8 == LANES - 1, t_full[:, g * group - LANES : g * group], edge)
        if g < groups - 1:
            edge = jnp.where(lane8 == 0, t_full[:, (g + 1) * group : (g + 1) * group + LANES], edge)
        edges.append(edge)
    parts = split(jnp.concatenate([to_groups(t_full, group), jnp.concatenate(edges, axis=0)], axis=1), 2)
    size = groups * KCOEF
    wide = dot(jnp.concatenate(parts, axis=0), colw[0])
    wide = wide[:size] + wide[size:] + dot(parts[0], colw[1])
    desc = from_groups(wide[:, :LANES], groups).astype(BF16)
    dx = from_groups(wide[:, LANES:], groups)
    comm[me] = desc

    @pl.when(mt == 0)
    def _():
        pl.semaphore_wait(barrier, tiles * (near_last - me) + tiles - 1)
        for side in range(1, tiles):
            pl.semaphore_signal(near_ok, inc=1, device_id={"tile": side}, device_id_type=MESH)

    @pl.when(mt > 0)
    def _():
        pl.semaphore_wait(near_ok, 1)


    def desc_copy(target):
        return pltpu.make_async_remote_copy(
            src_ref=comm.at[me], dst_ref=comm.at[me], send_sem=ssem.at[target], recv_sem=rsem.at[me],
            device_id={"sec": target}, device_id_type=MESH,
        )

    def send_desc(step, carry):
        desc_copy(me + 1 + step).start()
        return carry

    lax.fori_loop(0, last - me, send_desc, 0)

    to_next = pltpu.make_async_remote_copy(
        src_ref=xext.at[pl.ds(rows, PAD)], dst_ref=xext.at[pl.ds(0, PAD)],
        send_sem=halo_ssem.at[0], recv_sem=halo_rsem.at[0],
        device_id={"tile": jnp.minimum(mt + 1, tiles - 1)}, device_id_type=MESH,
    )
    to_last = pltpu.make_async_remote_copy(
        src_ref=xext.at[pl.ds(PAD, PAD)], dst_ref=xext.at[pl.ds(PAD + rows, PAD)],
        send_sem=halo_ssem.at[1], recv_sem=halo_rsem.at[1],
        device_id={"tile": jnp.maximum(mt - 1, 0)}, device_id_type=MESH,
    )

    @pl.when(mt < tiles - 1)
    def _():
        to_next.start()

    @pl.when(mt > 0)
    def _():
        to_last.start()

    @pl.when(mt == 0)
    def _():
        xext[0:PAD, :] = jnp.zeros((PAD, cols), BF16)

    @pl.when(mt == tiles - 1)
    def _():
        xext[PAD + rows : 2 * PAD + rows, :] = jnp.zeros((PAD, cols), BF16)

    fetches[3].wait()

    @pl.when(mt < tiles - 1)
    def _():
        to_last.wait_recv()

    @pl.when(mt > 0)
    def _():
        to_next.wait_recv()

    part = dot(second_ref[...], xext[...])
    t_full = part[0:KCOEF] + part[KCOEF : 2 * KCOEF]
    for j in range(4):
        begin = 2 * KCOEF + j * sums
        sums_ref[j] = part[begin : begin + sums]
    for v in range(blocks):
        at = slice(v * LANES, (v + 1) * LANES)
        xtall[v] = xext[:, at].astype(F32)
    parts = split(to_groups(t_full, group), 2)
    wide = dot(jnp.concatenate(parts, axis=0), colw[0, 0:group, 0:LANES])
    dy = from_groups(wide[:size] + wide[size:] + dot(parts[0], colw[1, 0:group, 0:LANES]), groups)

    def row_total(value):
        for step in (4, 2, 1):
            value = value + pltpu.roll(value, step, 0)
        return value

    fetches[6].wait()

    def narrow(values):
        left = jnp.concatenate(values, axis=0)
        size = left.shape[0]
        wide = dot(jnp.concatenate(split(left, 3), axis=0), compact[...])
        total = wide[:size] + (wide[size : 2 * size] + wide[2 * size :])
        step = size // len(values)
        return [row_total(total[i * step : (i + 1) * step]) for i in range(len(values))]

    gxx, gxy, gyy = narrow([dx * dx, dx * dy, dy * dy])
    gxx = gxx + REG
    gyy = gyy + REG
    scale = 1.0 / (gxx * gyy - gxy * gxy)

    fetches[4].wait()
    fetches[5].wait()

    def wait_desc(q, carry):
        pltpu.make_async_remote_copy(
            src_ref=comm.at[q], dst_ref=comm.at[q], send_sem=ssem.at[q], recv_sem=rsem.at[q],
            device_id={"sec": q}, device_id_type=MESH,
        ).wait_recv()
        return carry

    lax.fori_loop(first, me, wait_desc, 0)

    keyref = comm[kf_ref[0]].astype(F32)
    predref = jnp.where(me > 0, comm[jnp.maximum(me - 1, 0)].astype(F32), 0.0)
    diff = 0.5 * (keyref + predref) - desc.astype(F32)
    bx, by = narrow([dx * diff, dy * diff])
    ux = (gyy * bx - gxy * by) * scale
    uy = (gxx * by - gxy * bx) * scale
    field_ref[0, 0] = ux[0:1, 0 : cols // PATCH]
    field_ref[0, 1] = uy[0:1, 0 : cols // PATCH]

    which = lax.broadcasted_iota(jnp.int32, (KCOEF, LANES), 0)
    picked = None
    for k, weight in enumerate(taps(ux) + taps(uy)):
        picked = weight if picked is None else jnp.where(which == k, weight, picked)
    picked_taps = picked
    half = jnp.where(lane8 < PATCH, 0, 1)
    for v in range(blocks):
        weights[:, v * LANES : (v + 1) * LANES] = jnp.take_along_axis(picked, half + 2 * v, axis=1)

    def combine(terms, first, at):
        times = terms[0].shape[0] // KCOEF
        total = None
        for k, term in enumerate(terms):
            factor = jnp.broadcast_to(weights[first + k : first + k + 1, at], (KCOEF, term.shape[1]))
            term = stacked(factor, times) * term
            total = term if total is None else total + term
        return total

    for v in range(blocks):
        at = slice(v * LANES, (v + 1) * LANES)
        vsum[:, LANES + v * LANES : 2 * LANES + v * LANES] = combine([sums_ref[k, :, at] for k in range(4)], 4, at)

    def turned(ref, v, count):
        left, center, right = (ref[0:count, pl.ds(pl.multiple_of((v + i) * LANES, LANES), LANES)] for i in range(3))
        lane = lax.broadcasted_iota(jnp.int32, (count, LANES), 1)
        even = jnp.where(lane >= 96, left, center)
        odd = jnp.where(lane < 32, right, center)
        return (
            pltpu.roll(even, (LANES - off_ref[0, 2 * v]) & (LANES - 1), 1),
            pltpu.roll(odd, (LANES - off_ref[0, 2 * v + 1]) & (LANES - 1), 1),
        )

    for v in range(0, blocks, 2):
        pairs = [turned(vsum, v + i, sums) for i in range(2)]
        for i in range(2):
            lhs_s[v * sums : (v + 2) * sums, i * LANES : (i + 1) * LANES] = jnp.concatenate(
                [pair[i] for pair in pairs], axis=0
            ).astype(BF16)
    fetches[7].wait()
    slots = LANES // BOX
    per = LANES // slots
    slot = lane8 // slots
    for m in range(blocks // per):
        wide = dot(lhs_s[m * per * sums : (m + 1) * per * sums, :], pooled_ref[...])
        picked = None
        for i in range(per):
            piece = wide[i * sums : (i + 1) * sums]
            piece = [piece[:, j * LANES : (j + 1) * LANES] for j in range(4)]
            picked = piece if i == 0 else [jnp.where(slot == i, new, old) for new, old in zip(piece, picked)]
        at = slice(m * LANES, (m + 1) * LANES)
        small = jnp.take_along_axis(picked_taps, lane8 // BOX + m * slots, axis=1)
        total = None
        for k in range(4):
            term = jnp.broadcast_to(small[k : k + 1], (sums, LANES)) * picked[k]
            total = term if total is None else total + term
        block_ref[:, at] = total
        bsend[:, at] = total.astype(BF16)

    def block_copy(target):
        return pltpu.make_async_remote_copy(
            src_ref=bsend, dst_ref=brecv.at[target - me - 1], send_sem=bssem.at[target - me - 1],
            recv_sem=brsem.at[target - me - 1], device_id={"sec": target}, device_id_type=MESH,
        )

    def send_block(target, carry):
        block_copy(target).start()
        return carry

    nearest = jnp.minimum(near_last, me + reach)
    lax.fori_loop(0, nearest - me, lambda i, carry: send_block(nearest - i, carry), 0)

    @pl.when(far_last > near_last)
    def _():
        @pl.when(mt == tiles - 1)
        def _():
            pl.semaphore_wait(barrier, tiles * (far_last - near_last))
            for side in range(tiles - 1):
                pl.semaphore_signal(far_ok, inc=1, device_id={"tile": side}, device_id_type=MESH)

        @pl.when(mt < tiles - 1)
        def _():
            pl.semaphore_wait(far_ok, 1)

        lax.fori_loop(0, far_last - near_last, lambda i, carry: send_block(far_last - i, carry), 0)

    fetches[8].wait()

    def vertical(v):
        at = slice(v * LANES, (v + 1) * LANES)
        total = combine([xtall[v, PAD + k : PAD + k + rows] for k in range(-1, 3)], 4, at)
        vert[:, (v + 1) * LANES : (v + 2) * LANES] = total.astype(BF16)

    def turn(v):
        even, odd = turned(vert, v, rows)
        lhs[v * rows : (v + 1) * rows, 0:LANES] = even
        lhs[v * rows : (v + 1) * rows, LANES : 2 * LANES] = odd

    lane64 = lax.broadcasted_iota(jnp.int32, (rows, LANES), 1)

    def across(g):
        wide = dot(lhs[g * CHUNK * rows : (g + 1) * CHUNK * rows, :], outer_ref[...])
        for i in range(CHUNK):
            v = g * CHUNK + i
            at = slice(v * LANES, (v + 1) * LANES)
            even = lhs[v * rows : (v + 1) * rows, 0:LANES]
            odd = lhs[v * rows : (v + 1) * rows, LANES : 2 * LANES]
            center = jnp.where(lane64 < PATCH, even, odd)
            after = pltpu.roll(jnp.where(((lane64 - 1) & (LANES - 1)) < PATCH, even, odd), LANES - 1, 1)
            piece = wide[i * rows : (i + 1) * rows]
            terms = [piece[:, :LANES], center.astype(F32), after.astype(F32), piece[:, LANES:]]
            obuf[0, :, at] = combine(terms, 0, at).astype(BF16)

    steps = blocks // CHUNK
    vertical(0)
    for step in range(steps + 2):
        if 0 <= step - 2:
            across(step - 2)
        if 0 <= step - 1 < steps:
            for i in range(CHUNK):
                turn((step - 1) * CHUNK + i)
        if step < steps:
            for i in range(CHUNK):
                if step * CHUNK + i + 1 < blocks:
                    vertical(step * CHUNK + i + 1)

    def sent_desc(target, carry):
        desc_copy(target).wait_send()
        return carry

    def sent_block(target, carry):
        block_copy(target).wait_send()
        return carry

    lax.fori_loop(me + 1, last + 1, sent_desc, 0)
    lax.fori_loop(me + 1, jnp.minimum(me + reach, n - 1) + 1, sent_block, 0)

    @pl.when(mt < tiles - 1)
    def _():
        to_next.wait_send()

    @pl.when(mt > 0)
    def _():
        to_last.wait_send()

    share = 1.0 / (BOX * BOX * WIN)
    pyr_ref[0] = block_ref[...] * share
    for d in range(reach, 0, -1):
        @pl.when(me >= d)
        def _():
            pltpu.make_async_remote_copy(
                src_ref=bsend, dst_ref=brecv.at[d - 1], send_sem=bssem.at[d - 1], recv_sem=brsem.at[d - 1],
                device_id={"sec": jnp.maximum(me - d, 0)}, device_id_type=MESH,
            ).wait_recv()
            pyr_ref[0] = pyr_ref[0] + brecv[d - 1].astype(F32) * share


def write_out(a, b, c, a_out, b_out, c_out, sem):
    copies = [
        pltpu.make_async_copy(source, target, sem.at[i])
        for i, (source, target) in enumerate(((a, a_out), (b, b_out), (c, c_out)))
    ]
    for copy in copies:
        copy.start()
    for copy in copies:
        copy.wait()


def body(n, tiles, image, keyframe, offsets):
    _, rows, cols = image.shape
    first, second = row_tables(rows)
    piece, ends = column_tables()
    outer, pooled = across_tables()
    ext = rows + 2 * PAD
    sums = rows // BOX
    coefs = cols // PATCH * KCOEF
    group = LANES // KCOEF * PATCH
    compact = gather_table(coefs)
    constants = (first, second, piece, ends, outer, pooled, compact)
    vmem = pl.BlockSpec(memory_space=pltpu.VMEM)
    hbm = pl.BlockSpec(memory_space=pltpu.HBM)
    dma = pltpu.SemaphoreType.DMA
    results = pl.pallas_call(
        functools.partial(kernel, n, tiles),
        out_shape=(
            pltpu.VMEM(image.shape, BF16),
            pltpu.VMEM((1, 2, 1, cols // PATCH), F32),
            pltpu.VMEM((1, sums, cols // BOX), F32),
        ),
        in_specs=[hbm] * (3 + len(constants)),
        out_specs=(vmem, vmem, vmem),
        scratch_shapes=[
            pltpu.SMEM((1,), jnp.int32),
            pltpu.SMEM((1, cols // PATCH), jnp.int32),
            *[pltpu.VMEM(value.shape, BF16) for value in constants],
            pltpu.VMEM((ext, cols), BF16),
            pltpu.VMEM((cols // LANES, ext, LANES), F32),
            pltpu.VMEM((2, group + LANES, 2 * LANES), BF16),
            pltpu.VMEM((n, KCOEF, coefs), BF16),
            pltpu.VMEM((4, sums, cols), F32),
            pltpu.VMEM((sums, cols + 2 * LANES), F32),
            pltpu.VMEM((cols // LANES * sums, 2 * LANES), BF16),
            pltpu.VMEM((rows, cols + 2 * LANES), BF16),
            pltpu.VMEM((cols // LANES * rows, 2 * LANES), BF16),
            pltpu.VMEM((KCOEF, cols), F32),
            pltpu.VMEM((WIN - 1, sums, cols // BOX), BF16),
            pltpu.VMEM((sums, cols // BOX), BF16),
            pltpu.VMEM((sums, cols // BOX), F32),
            dma,
            dma((9,)),
            dma((2,)),
            dma((2,)),
            dma((n,)),
            dma((n,)),
            dma((WIN - 1,)),
            dma((WIN - 1,)),
            pltpu.SemaphoreType.REGULAR,
            pltpu.SemaphoreType.REGULAR,
        ],
        compiler_params=pltpu.CompilerParams(collective_id=0, has_side_effects=True),
    )(keyframe, offsets, *[jnp.asarray(value) for value in constants], image)
    return pl.pallas_call(
        write_out,
        out_shape=tuple(jax.ShapeDtypeStruct(r.shape, r.dtype) for r in results),
        in_specs=[vmem] * 3,
        out_specs=(hbm,) * 3,
        scratch_shapes=[dma((3,))],
    )(*[pltpu.with_memory_space_constraint(r, pltpu.VMEM) for r in results])


def solution(mesh):
    return jax.shard_map(
        functools.partial(body, mesh.shape["sec"], mesh.shape["tile"]),
        mesh=mesh,
        in_specs=(P(("slab", "sec"), "tile", None), P(("slab", "sec")), P(("slab", "sec"), None)),
        out_specs=(
            P(("slab", "sec"), "tile", None),
            P(("slab", "sec"), None, "tile", None),
            P(("slab", "sec"), "tile", None),
        ),
        check_vma=False,
    )
```

```python
import functools

import jax
import jax.numpy as jnp
import ml_dtypes
import numpy as np
from jax import lax
from jax.experimental import pallas as pl
from jax.experimental.pallas import tpu as pltpu
from jax.sharding import PartitionSpec as P

PATCH = 64
KCOEF = 8
WIN = 8
REG = 4.0
BOX = 8
LANES = 128
PAD = 16
CHUNK = 8
MESH = pl.DeviceIdType.MESH
F32 = jnp.float32
BF16 = jnp.bfloat16


def np_split(value, terms):
    parts = []
    rest = np.asarray(value, np.float64)
    for _ in range(terms):
        part = rest.astype(np.float32).astype(ml_dtypes.bfloat16)
        parts.append(part)
        rest = rest - part.astype(np.float64)
    return parts


def cosines():
    index = np.arange(PATCH, dtype=np.float64)
    order = np.arange(KCOEF, dtype=np.float64)
    table = np.sqrt(2.0 / PATCH) * np.cos(np.pi * (index[None, :] + 0.5) * order[:, None] / PATCH)
    table = table * np.where(order == 0, np.sqrt(0.5), 1.0)[:, None]
    return table.astype(np.float32).astype(np.float64)


def row_tables(rows):
    table = cosines()
    ext = rows + 2 * PAD
    first = np.concatenate(np_split(table, 2), axis=0)
    slope = np.zeros((KCOEF, ext))
    slope[:, PAD + 1 : PAD + 1 + rows] += 0.5 * table
    slope[:, PAD - 1 : PAD - 1 + rows] -= 0.5 * table
    second = np_split(slope, 2)
    for k in range(-1, 3):
        sums = np.zeros((rows // BOX, ext))
        for r in range(rows):
            sums[r // BOX, PAD + r + k] = 1.0
        second.append(sums.astype(ml_dtypes.bfloat16))
    return first, np.concatenate(second, axis=0)


def column_tables():
    table = cosines()
    slope = np.zeros((PATCH, KCOEF))
    slope[1:] += 0.5 * table.T[:-1]
    slope[:-1] -= 0.5 * table.T[1:]
    times = (1, LANES // KCOEF)
    pieces = []
    for both in (np_split(np.concatenate([np.tile(table.T, times), np.tile(slope, times)], axis=1), 2)):
        pieces.append(both)
    ends = np.zeros((16, LANES))
    ends[0] = np.tile(-0.5 * table[:, 0], LANES // KCOEF)
    ends[1] = np.tile(0.5 * table[:, PATCH - 1], LANES // KCOEF)
    return np.stack(pieces), np.stack(np_split(ends, 2))


def across_tables():
    shift = np.zeros((2 * LANES, 4, LANES))
    for k in range(-1, 3):
        for c in range(LANES):
            shift[(0 if c < PATCH else LANES) + (c + k) % LANES, k + 1, c] = 1.0
    slots = LANES // BOX
    pooled = shift.reshape(2 * LANES, 4, slots, BOX).sum(axis=3)
    pooled = np.tile(pooled, (1, 1, LANES // slots)).reshape(2 * LANES, 4 * LANES)
    outer = shift[:, (0, 3)].reshape(2 * LANES, 2 * LANES)
    return outer.astype(ml_dtypes.bfloat16), pooled.astype(ml_dtypes.bfloat16)


def gather_table(coefs):
    found = np.zeros((coefs, LANES))
    for i in range(coefs):
        found[i, i // KCOEF :: coefs // KCOEF] = 1.0
    return found.astype(ml_dtypes.bfloat16)


def split(value, terms):
    parts = []
    for _ in range(terms):
        part = value.astype(BF16)
        parts.append(part)
        value = value - part.astype(F32)
    return parts


def dot(a, b):
    return jnp.dot(a, b, preferred_element_type=F32)


def to_groups(value, width):
    count = value.shape[1] // width
    return jnp.concatenate([value[:, g * width : (g + 1) * width] for g in range(count)], axis=0)


def from_groups(value, count):
    rows = value.shape[0] // count
    return jnp.concatenate([value[g * rows : (g + 1) * rows] for g in range(count)], axis=1)


def taps(shift):
    return (
        -shift * (shift - 1.0) * (shift - 2.0) * (1.0 / 6.0),
        (shift + 1.0) * (shift - 1.0) * (shift - 2.0) * 0.5,
        -(shift + 1.0) * shift * (shift - 2.0) * 0.5,
        (shift + 1.0) * shift * (shift - 1.0) * (1.0 / 6.0),
    )


def stacked(value, times):
    return value if times == 1 else jnp.concatenate([value] * times, axis=0)


def kernel(
    n, tiles, kf_hbm, off_hbm, first_hbm, second_hbm, piece_hbm, ends_hbm, outer_hbm, pooled_hbm, compact_hbm, x_hbm,
    obuf, field_ref, pyr_ref,
    kf_ref, off_ref, first_ref, second_ref, piece_ref, ends_ref, outer_ref, pooled_ref, compact,
    xext, xtall, colw, comm, sums_ref, vsum, lhs_s, vert, lhs, weights, brecv, bsend, block_ref,
    load_sem, table_sem, halo_ssem, halo_rsem, ssem, rsem, bssem, brsem, near_ok, far_ok, pair_ok, late_ok,
):
    me = lax.axis_index("sec")
    mt = lax.axis_index("tile")
    _, rows, cols = obuf.shape
    group = LANES // KCOEF * PATCH
    groups = cols // group
    blocks = cols // LANES
    sums = rows // BOX

    barrier = pltpu.get_barrier_semaphore()
    load = pltpu.make_async_copy(x_hbm.at[0], xext.at[pl.ds(PAD, rows)], load_sem)
    fetches = [
        pltpu.make_async_copy(source, target, table_sem.at[i])
        for i, (source, target) in enumerate((
            (piece_hbm, piece_ref), (ends_hbm, ends_ref), (first_hbm, first_ref), (second_hbm, second_ref),
            (kf_hbm, kf_ref), (off_hbm, off_ref), (compact_hbm, compact), (pooled_hbm, pooled_ref),
            (outer_hbm, outer_ref),
        ))
    ]
    reach = min(WIN, n) - 1
    middle = n // 2 - 1
    start = jnp.where(me >= n - 1, n - 1, jnp.where(me >= middle, middle, 0))
    stop = jnp.where(me < middle, middle, n - 1)
    first = jnp.maximum(jnp.minimum(start, me - 1), 0)
    last = jnp.minimum(jnp.maximum(stop - 1, me + 1), n - 1)
    near_first = first
    near_last = last
    far_first = jnp.minimum(jnp.maximum(me - reach, 0), near_first)
    far_last = jnp.where(me < middle, jnp.maximum(jnp.minimum(me + reach, n - 1), near_last), near_last)
    late_first = max(middle, n - 1 - reach)
    late_count = max(n - 2 - late_first, 0)
    late = (me >= late_first) & (me < n - 2)

    def greet(side, q, carry):
        pl.semaphore_signal(barrier, inc=1, device_id={"sec": q, "tile": side}, device_id_type=MESH)
        return carry

    lax.fori_loop(near_first, me, functools.partial(greet, 0), 0)
    lax.fori_loop(far_first, jnp.minimum(near_first, middle), functools.partial(greet, tiles - 1), 0)

    @pl.when(late)
    def _():
        greet(mt, n - 1, 0)

    far = far_last > near_last

    @pl.when(far & (mt > 0))
    def _():
        pl.semaphore_signal(barrier, inc=1, device_id={"tile": 0}, device_id_type=MESH)

    @pl.when(jnp.logical_not(far) & (mt == 0))
    def _():
        for side in range(1, tiles):
            pl.semaphore_signal(barrier, inc=1, device_id={"tile": side}, device_id_type=MESH)

    for fetch in fetches[:3]:
        fetch.start()
    load.start()
    for fetch in fetches[3:7]:
        fetch.start()

    for edge in (0, blocks + 1):
        at = slice(edge * LANES, (edge + 1) * LANES)
        vert[:, at] = jnp.zeros((rows, LANES), BF16)
        vsum[:, at] = jnp.zeros((sums, LANES), F32)

    fetches[0].wait()
    fetches[1].wait()
    own = lax.broadcasted_iota(jnp.int32, (PATCH, LANES), 1) // KCOEF
    row_of = lax.broadcasted_iota(jnp.int32, (PATCH, LANES), 0)

    def build_columns(p, carry):
        at = pl.ds(pl.multiple_of(p * PATCH, PATCH), PATCH)
        for term in range(2):
            piece = piece_ref[term].astype(F32)
            ends = ends_ref[term].astype(F32)
            colw[term, at, 0:LANES] = jnp.where(own == p, piece[:, :LANES], 0.0).astype(BF16)
            slope = jnp.where(own == p, piece[:, LANES:], 0.0)
            slope = jnp.where((own == p + 1) & (row_of == PATCH - 1), ends[0:1], slope)
            slope = jnp.where((own == p - 1) & (row_of == 0), ends[1:2], slope)
            colw[term, at, LANES : 2 * LANES] = slope.astype(BF16)
        return carry

    lax.fori_loop(0, group // PATCH, build_columns, 0)
    side = lax.broadcasted_iota(jnp.int32, (LANES, LANES), 1) // KCOEF
    deep = lax.broadcasted_iota(jnp.int32, (LANES, LANES), 0)
    for term in range(2):
        ends = ends_ref[term].astype(F32)
        tail = jnp.where((side == LANES // KCOEF - 1) & (deep == 0), ends[1:2], 0.0)
        tail = jnp.where((side == 0) & (deep == LANES - 1), ends[0:1], tail)
        colw[term, group : group + LANES, 0:LANES] = jnp.zeros((LANES, LANES), BF16)
        colw[term, group : group + LANES, LANES : 2 * LANES] = tail.astype(BF16)

    fetches[2].wait()
    load.wait()
    for fetch in fetches[7:]:
        fetch.start()

    to_next = pltpu.make_async_remote_copy(
        src_ref=xext.at[pl.ds(rows, PAD)], dst_ref=xext.at[pl.ds(0, PAD)],
        send_sem=halo_ssem.at[0], recv_sem=halo_rsem.at[0],
        device_id={"tile": jnp.minimum(mt + 1, tiles - 1)}, device_id_type=MESH,
    )
    to_last = pltpu.make_async_remote_copy(
        src_ref=xext.at[pl.ds(PAD, PAD)], dst_ref=xext.at[pl.ds(PAD + rows, PAD)],
        send_sem=halo_ssem.at[1], recv_sem=halo_rsem.at[1],
        device_id={"tile": jnp.maximum(mt - 1, 0)}, device_id_type=MESH,
    )

    def send_halo():
        @pl.when(mt < tiles - 1)
        def _():
            to_next.start()

        @pl.when(mt > 0)
        def _():
            to_last.start()

    @pl.when(jnp.logical_not(far))
    def _():
        @pl.when(mt > 0)
        def _():
            pl.semaphore_wait(barrier, 1 + jnp.where(me == n - 1, late_count, 0))
            pl.semaphore_signal(pair_ok, inc=1, device_id={"tile": 0}, device_id_type=MESH)

        @pl.when(mt == 0)
        def _():
            pl.semaphore_wait(pair_ok, tiles - 1)

        send_halo()

    if late_count > 0:
        @pl.when(me == n - 1)
        def _():
            @pl.when(mt == 0)
            def _():
                pl.semaphore_wait(barrier, late_count)

            for q in range(late_first, n - 2):
                pl.semaphore_signal(late_ok, inc=1, device_id={"sec": q}, device_id_type=MESH)

    part = dot(first_ref[...], xext[PAD : PAD + rows, :])
    t_full = part[0:KCOEF] + part[KCOEF : 2 * KCOEF]
    lane8 = lax.broadcasted_iota(jnp.int32, (KCOEF, LANES), 1)
    edges = []
    for g in range(groups):
        edge = jnp.zeros((KCOEF, LANES), F32)
        if g > 0:
            edge = jnp.where(lane8 == LANES - 1, t_full[:, g * group - LANES : g * group], edge)
        if g < groups - 1:
            edge = jnp.where(lane8 == 0, t_full[:, (g + 1) * group : (g + 1) * group + LANES], edge)
        edges.append(edge)
    parts = split(jnp.concatenate([to_groups(t_full, group), jnp.concatenate(edges, axis=0)], axis=1), 2)
    size = groups * KCOEF
    wide = dot(jnp.concatenate(parts, axis=0), colw[0])
    wide = wide[:size] + wide[size:] + dot(parts[0], colw[1])
    desc = from_groups(wide[:, :LANES], groups).astype(BF16)
    dx = from_groups(wide[:, LANES:], groups)
    comm[me] = desc

    @pl.when(mt == 0)
    def _():
        count = tiles * (near_last - me) + jnp.where(far, tiles - 1, 0)

        @pl.when(count > 0)
        def _():
            pl.semaphore_wait(barrier, count)

        for side in range(1, tiles):
            pl.semaphore_signal(near_ok, inc=1, device_id={"tile": side}, device_id_type=MESH)

    @pl.when(mt > 0)
    def _():
        pl.semaphore_wait(near_ok, 1)


    def desc_copy(target):
        return pltpu.make_async_remote_copy(
            src_ref=comm.at[me], dst_ref=comm.at[me], send_sem=ssem.at[target], recv_sem=rsem.at[me],
            device_id={"sec": target}, device_id_type=MESH,
        )

    def send_desc(step, carry):
        desc_copy(me + 1 + step).start()
        return carry

    lax.fori_loop(0, last - me, send_desc, 0)

    pl.when(far)(send_halo)

    @pl.when(mt == 0)
    def _():
        xext[0:PAD, :] = jnp.zeros((PAD, cols), BF16)

    @pl.when(mt == tiles - 1)
    def _():
        xext[PAD + rows : 2 * PAD + rows, :] = jnp.zeros((PAD, cols), BF16)

    fetches[3].wait()

    @pl.when(mt < tiles - 1)
    def _():
        to_last.wait_recv()

    @pl.when(mt > 0)
    def _():
        to_next.wait_recv()

    part = dot(second_ref[...], xext[...])
    t_full = part[0:KCOEF] + part[KCOEF : 2 * KCOEF]
    for j in range(4):
        begin = 2 * KCOEF + j * sums
        sums_ref[j] = part[begin : begin + sums]
    for v in range(blocks):
        at = slice(v * LANES, (v + 1) * LANES)
        xtall[v] = xext[:, at].astype(F32)
    parts = split(to_groups(t_full, group), 2)
    wide = dot(jnp.concatenate(parts, axis=0), colw[0, 0:group, 0:LANES])
    dy = from_groups(wide[:size] + wide[size:] + dot(parts[0], colw[1, 0:group, 0:LANES]), groups)

    def row_total(value):
        for step in (4, 2, 1):
            value = value + pltpu.roll(value, step, 0)
        return value

    fetches[6].wait()

    def narrow(values):
        left = jnp.concatenate(values, axis=0)
        size = left.shape[0]
        wide = dot(jnp.concatenate(split(left, 3), axis=0), compact[...])
        total = wide[:size] + (wide[size : 2 * size] + wide[2 * size :])
        step = size // len(values)
        return [row_total(total[i * step : (i + 1) * step]) for i in range(len(values))]

    gxx, gxy, gyy = narrow([dx * dx, dx * dy, dy * dy])
    gxx = gxx + REG
    gyy = gyy + REG
    scale = 1.0 / (gxx * gyy - gxy * gxy)

    fetches[4].wait()
    fetches[5].wait()

    def wait_desc(q, carry):
        pltpu.make_async_remote_copy(
            src_ref=comm.at[q], dst_ref=comm.at[q], send_sem=ssem.at[q], recv_sem=rsem.at[q],
            device_id={"sec": q}, device_id_type=MESH,
        ).wait_recv()
        return carry

    lax.fori_loop(first, me, wait_desc, 0)

    keyref = comm[kf_ref[0]].astype(F32)
    predref = jnp.where(me > 0, comm[jnp.maximum(me - 1, 0)].astype(F32), 0.0)
    diff = 0.5 * (keyref + predref) - desc.astype(F32)
    bx, by = narrow([dx * diff, dy * diff])
    ux = (gyy * bx - gxy * by) * scale
    uy = (gxx * by - gxy * bx) * scale
    field_ref[0, 0] = ux[0:1, 0 : cols // PATCH]
    field_ref[0, 1] = uy[0:1, 0 : cols // PATCH]

    which = lax.broadcasted_iota(jnp.int32, (KCOEF, LANES), 0)
    picked = None
    for k, weight in enumerate(taps(ux) + taps(uy)):
        picked = weight if picked is None else jnp.where(which == k, weight, picked)
    picked_taps = picked
    half = jnp.where(lane8 < PATCH, 0, 1)
    for v in range(blocks):
        weights[:, v * LANES : (v + 1) * LANES] = jnp.take_along_axis(picked, half + 2 * v, axis=1)

    def combine(terms, first, at):
        times = terms[0].shape[0] // KCOEF
        total = None
        for k, term in enumerate(terms):
            factor = jnp.broadcast_to(weights[first + k : first + k + 1, at], (KCOEF, term.shape[1]))
            term = stacked(factor, times) * term
            total = term if total is None else total + term
        return total

    for v in range(blocks):
        at = slice(v * LANES, (v + 1) * LANES)
        vsum[:, LANES + v * LANES : 2 * LANES + v * LANES] = combine([sums_ref[k, :, at] for k in range(4)], 4, at)

    def turned(ref, v, count):
        left, center, right = (ref[0:count, pl.ds(pl.multiple_of((v + i) * LANES, LANES), LANES)] for i in range(3))
        lane = lax.broadcasted_iota(jnp.int32, (count, LANES), 1)
        even = jnp.where(lane >= 96, left, center)
        odd = jnp.where(lane < 32, right, center)
        return (
            pltpu.roll(even, (LANES - off_ref[0, 2 * v]) & (LANES - 1), 1),
            pltpu.roll(odd, (LANES - off_ref[0, 2 * v + 1]) & (LANES - 1), 1),
        )

    for v in range(0, blocks, 2):
        pairs = [turned(vsum, v + i, sums) for i in range(2)]
        for i in range(2):
            lhs_s[v * sums : (v + 2) * sums, i * LANES : (i + 1) * LANES] = jnp.concatenate(
                [pair[i] for pair in pairs], axis=0
            ).astype(BF16)
    fetches[7].wait()
    slots = LANES // BOX
    per = LANES // slots
    slot = lane8 // slots
    for m in range(blocks // per):
        if m % 2 == 0:
            whole = dot(lhs_s[m * per * sums : (m + 2) * per * sums, :], pooled_ref[...])
        wide = whole[m % 2 * per * sums : (m % 2 + 1) * per * sums]
        picked = None
        for i in range(per):
            piece = wide[i * sums : (i + 1) * sums]
            piece = [piece[:, j * LANES : (j + 1) * LANES] for j in range(4)]
            picked = piece if i == 0 else [jnp.where(slot == i, new, old) for new, old in zip(piece, picked)]
        at = slice(m * LANES, (m + 1) * LANES)
        small = jnp.take_along_axis(picked_taps, lane8 // BOX + m * slots, axis=1)
        total = None
        for k in range(4):
            term = jnp.broadcast_to(small[k : k + 1], (sums, LANES)) * picked[k]
            total = term if total is None else total + term
        block_ref[:, at] = total
        bsend[:, at] = total.astype(BF16)

    def block_copy(target):
        return pltpu.make_async_remote_copy(
            src_ref=bsend, dst_ref=brecv.at[target - me - 1], send_sem=bssem.at[target - me - 1],
            recv_sem=brsem.at[target - me - 1], device_id={"sec": target}, device_id_type=MESH,
        )

    def send_block(target, carry):
        block_copy(target).start()
        return carry

    nearest = jnp.minimum(near_last, me + reach)
    lax.fori_loop(0, nearest - me, lambda i, carry: send_block(nearest - i, carry), 0)

    @pl.when(late)
    def _():
        pl.semaphore_wait(late_ok, 1)
        send_block(n - 1, 0)

    @pl.when(far)
    def _():
        @pl.when(mt == tiles - 1)
        def _():
            pl.semaphore_wait(barrier, tiles * (far_last - near_last))
            for side in range(tiles - 1):
                pl.semaphore_signal(far_ok, inc=1, device_id={"tile": side}, device_id_type=MESH)

        @pl.when(mt < tiles - 1)
        def _():
            pl.semaphore_wait(far_ok, 1)

        lax.fori_loop(0, far_last - near_last, lambda i, carry: send_block(far_last - i, carry), 0)

    fetches[8].wait()

    def vertical(v):
        at = slice(v * LANES, (v + 1) * LANES)
        total = combine([xtall[v, PAD + k : PAD + k + rows] for k in range(-1, 3)], 4, at)
        vert[:, (v + 1) * LANES : (v + 2) * LANES] = total.astype(BF16)

    def turn(v):
        even, odd = turned(vert, v, rows)
        lhs[v * rows : (v + 1) * rows, 0:LANES] = even
        lhs[v * rows : (v + 1) * rows, LANES : 2 * LANES] = odd

    lane64 = lax.broadcasted_iota(jnp.int32, (rows, LANES), 1)

    def across(g):
        wide = dot(lhs[g * CHUNK * rows : (g + 1) * CHUNK * rows, :], outer_ref[...])
        for i in range(CHUNK):
            v = g * CHUNK + i
            at = slice(v * LANES, (v + 1) * LANES)
            even = lhs[v * rows : (v + 1) * rows, 0:LANES]
            odd = lhs[v * rows : (v + 1) * rows, LANES : 2 * LANES]
            center = jnp.where(lane64 < PATCH, even, odd)
            after = pltpu.roll(jnp.where(((lane64 - 1) & (LANES - 1)) < PATCH, even, odd), LANES - 1, 1)
            piece = wide[i * rows : (i + 1) * rows]
            terms = [piece[:, :LANES], center.astype(F32), after.astype(F32), piece[:, LANES:]]
            obuf[0, :, at] = combine(terms, 0, at).astype(BF16)

    steps = blocks // CHUNK
    vertical(0)
    for step in range(steps + 2):
        if 0 <= step - 2:
            across(step - 2)
        if 0 <= step - 1 < steps:
            for i in range(CHUNK):
                turn((step - 1) * CHUNK + i)
        if step < steps:
            for i in range(CHUNK):
                if step * CHUNK + i + 1 < blocks:
                    vertical(step * CHUNK + i + 1)

    def sent_desc(target, carry):
        desc_copy(target).wait_send()
        return carry

    def sent_block(target, carry):
        block_copy(target).wait_send()
        return carry

    lax.fori_loop(me + 1, last + 1, sent_desc, 0)
    lax.fori_loop(me + 1, jnp.minimum(me + reach, n - 1) + 1, sent_block, 0)

    @pl.when(mt < tiles - 1)
    def _():
        to_next.wait_send()

    @pl.when(mt > 0)
    def _():
        to_last.wait_send()

    share = 1.0 / (BOX * BOX * WIN)
    pyr_ref[0] = block_ref[...] * share
    for d in range(reach, 0, -1):
        @pl.when(me >= d)
        def _():
            pltpu.make_async_remote_copy(
                src_ref=bsend, dst_ref=brecv.at[d - 1], send_sem=bssem.at[d - 1], recv_sem=brsem.at[d - 1],
                device_id={"sec": jnp.maximum(me - d, 0)}, device_id_type=MESH,
            ).wait_recv()
            pyr_ref[0] = pyr_ref[0] + brecv[d - 1].astype(F32) * share


def write_out(a, b, c, a_out, b_out, c_out, sem):
    copies = [
        pltpu.make_async_copy(source, target, sem.at[i])
        for i, (source, target) in enumerate(((a, a_out), (b, b_out), (c, c_out)))
    ]
    for copy in copies:
        copy.start()
    for copy in copies:
        copy.wait()


def body(n, tiles, image, keyframe, offsets):
    _, rows, cols = image.shape
    first, second = row_tables(rows)
    piece, ends = column_tables()
    outer, pooled = across_tables()
    ext = rows + 2 * PAD
    sums = rows // BOX
    coefs = cols // PATCH * KCOEF
    group = LANES // KCOEF * PATCH
    compact = gather_table(coefs)
    constants = (first, second, piece, ends, outer, pooled, compact)
    vmem = pl.BlockSpec(memory_space=pltpu.VMEM)
    hbm = pl.BlockSpec(memory_space=pltpu.HBM)
    dma = pltpu.SemaphoreType.DMA
    results = pl.pallas_call(
        functools.partial(kernel, n, tiles),
        out_shape=(
            pltpu.VMEM(image.shape, BF16),
            pltpu.VMEM((1, 2, 1, cols // PATCH), F32),
            pltpu.VMEM((1, sums, cols // BOX), F32),
        ),
        in_specs=[hbm] * (3 + len(constants)),
        out_specs=(vmem, vmem, vmem),
        scratch_shapes=[
            pltpu.SMEM((1,), jnp.int32),
            pltpu.SMEM((1, cols // PATCH), jnp.int32),
            *[pltpu.VMEM(value.shape, BF16) for value in constants],
            pltpu.VMEM((ext, cols), BF16),
            pltpu.VMEM((cols // LANES, ext, LANES), F32),
            pltpu.VMEM((2, group + LANES, 2 * LANES), BF16),
            pltpu.VMEM((n, KCOEF, coefs), BF16),
            pltpu.VMEM((4, sums, cols), F32),
            pltpu.VMEM((sums, cols + 2 * LANES), F32),
            pltpu.VMEM((cols // LANES * sums, 2 * LANES), BF16),
            pltpu.VMEM((rows, cols + 2 * LANES), BF16),
            pltpu.VMEM((cols // LANES * rows, 2 * LANES), BF16),
            pltpu.VMEM((KCOEF, cols), F32),
            pltpu.VMEM((WIN - 1, sums, cols // BOX), BF16),
            pltpu.VMEM((sums, cols // BOX), BF16),
            pltpu.VMEM((sums, cols // BOX), F32),
            dma,
            dma((9,)),
            dma((2,)),
            dma((2,)),
            dma((n,)),
            dma((n,)),
            dma((WIN - 1,)),
            dma((WIN - 1,)),
            *[pltpu.SemaphoreType.REGULAR] * 4,
        ],
        compiler_params=pltpu.CompilerParams(collective_id=0, has_side_effects=True),
    )(keyframe, offsets, *[jnp.asarray(value) for value in constants], image)
    return pl.pallas_call(
        write_out,
        out_shape=tuple(jax.ShapeDtypeStruct(r.shape, r.dtype) for r in results),
        in_specs=[vmem] * 3,
        out_specs=(hbm,) * 3,
        scratch_shapes=[dma((3,))],
    )(*[pltpu.with_memory_space_constraint(r, pltpu.VMEM) for r in results])


def solution(mesh):
    return jax.shard_map(
        functools.partial(body, mesh.shape["sec"], mesh.shape["tile"]),
        mesh=mesh,
        in_specs=(P(("slab", "sec"), "tile", None), P(("slab", "sec")), P(("slab", "sec"), None)),
        out_specs=(
            P(("slab", "sec"), "tile", None),
            P(("slab", "sec"), None, "tile", None),
            P(("slab", "sec"), "tile", None),
        ),
        check_vma=False,
    )
```

```python
import functools

import jax
import jax.numpy as jnp
import ml_dtypes
import numpy as np
from jax import lax
from jax.experimental import pallas as pl
from jax.experimental.pallas import tpu as pltpu
from jax.sharding import PartitionSpec as P

PATCH = 64
KCOEF = 8
WIN = 8
REG = 4.0
BOX = 8
LANES = 128
PAD = 16
CHUNK = 8
MESH = pl.DeviceIdType.MESH
F32 = jnp.float32
BF16 = jnp.bfloat16


def np_split(value, terms):
    parts = []
    rest = np.asarray(value, np.float64)
    for _ in range(terms):
        part = rest.astype(np.float32).astype(ml_dtypes.bfloat16)
        parts.append(part)
        rest = rest - part.astype(np.float64)
    return parts


def cosines():
    index = np.arange(PATCH, dtype=np.float64)
    order = np.arange(KCOEF, dtype=np.float64)
    table = np.sqrt(2.0 / PATCH) * np.cos(np.pi * (index[None, :] + 0.5) * order[:, None] / PATCH)
    table = table * np.where(order == 0, np.sqrt(0.5), 1.0)[:, None]
    return table.astype(np.float32).astype(np.float64)


def row_tables(rows):
    table = cosines()
    ext = rows + 2 * PAD
    first = np.concatenate(np_split(table, 2), axis=0)
    slope = np.zeros((KCOEF, ext))
    slope[:, PAD + 1 : PAD + 1 + rows] += 0.5 * table
    slope[:, PAD - 1 : PAD - 1 + rows] -= 0.5 * table
    second = np_split(slope, 2)
    for k in range(-1, 3):
        sums = np.zeros((rows // BOX, ext))
        for r in range(rows):
            sums[r // BOX, PAD + r + k] = 1.0
        second.append(sums.astype(ml_dtypes.bfloat16))
    return first, np.concatenate(second, axis=0)


def column_tables():
    table = cosines()
    slope = np.zeros((PATCH, KCOEF))
    slope[1:] += 0.5 * table.T[:-1]
    slope[:-1] -= 0.5 * table.T[1:]
    times = (1, LANES // KCOEF)
    pieces = []
    for both in (np_split(np.concatenate([np.tile(table.T, times), np.tile(slope, times)], axis=1), 2)):
        pieces.append(both)
    ends = np.zeros((16, LANES))
    ends[0] = np.tile(-0.5 * table[:, 0], LANES // KCOEF)
    ends[1] = np.tile(0.5 * table[:, PATCH - 1], LANES // KCOEF)
    return np.stack(pieces), np.stack(np_split(ends, 2))


def across_tables():
    shift = np.zeros((2 * LANES, 4, LANES))
    for k in range(-1, 3):
        for c in range(LANES):
            shift[(0 if c < PATCH else LANES) + (c + k) % LANES, k + 1, c] = 1.0
    slots = LANES // BOX
    pooled = shift.reshape(2 * LANES, 4, slots, BOX).sum(axis=3)
    pooled = np.tile(pooled, (1, 1, LANES // slots)).reshape(2 * LANES, 4 * LANES)
    outer = shift[:, (0, 3)].reshape(2 * LANES, 2 * LANES)
    return outer.astype(ml_dtypes.bfloat16), pooled.astype(ml_dtypes.bfloat16)


def gather_table(coefs):
    found = np.zeros((coefs, LANES))
    for i in range(coefs):
        found[i, i // KCOEF :: coefs // KCOEF] = 1.0
    return found.astype(ml_dtypes.bfloat16)


def split(value, terms):
    parts = []
    for _ in range(terms):
        part = value.astype(BF16)
        parts.append(part)
        value = value - part.astype(F32)
    return parts


def dot(a, b):
    return jnp.dot(a, b, preferred_element_type=F32)


def to_groups(value, width):
    count = value.shape[1] // width
    return jnp.concatenate([value[:, g * width : (g + 1) * width] for g in range(count)], axis=0)


def from_groups(value, count):
    rows = value.shape[0] // count
    return jnp.concatenate([value[g * rows : (g + 1) * rows] for g in range(count)], axis=1)


def taps(shift):
    return (
        -shift * (shift - 1.0) * (shift - 2.0) * (1.0 / 6.0),
        (shift + 1.0) * (shift - 1.0) * (shift - 2.0) * 0.5,
        -(shift + 1.0) * shift * (shift - 2.0) * 0.5,
        (shift + 1.0) * shift * (shift - 1.0) * (1.0 / 6.0),
    )


def stacked(value, times):
    return value if times == 1 else jnp.concatenate([value] * times, axis=0)


def kernel(
    n, tiles, kf_hbm, off_hbm, first_hbm, second_hbm, piece_hbm, ends_hbm, outer_hbm, pooled_hbm, compact_hbm, x_hbm,
    obuf, field_ref, pyr_ref,
    kf_ref, off_ref, first_ref, second_ref, piece_ref, ends_ref, outer_ref, pooled_ref, compact,
    xext, xtall, colw, comm, sums_ref, vert, lhs, weights, brecv, bsend, block_ref,
    load_sem, table_sem, halo_ssem, halo_rsem, ssem, rsem, bssem, brsem, near_ok, far_ok, pair_ok, late_ok,
):
    me = lax.axis_index("sec")
    mt = lax.axis_index("tile")
    _, rows, cols = obuf.shape
    group = LANES // KCOEF * PATCH
    groups = cols // group
    blocks = cols // LANES
    sums = rows // BOX

    barrier = pltpu.get_barrier_semaphore()
    load = pltpu.make_async_copy(x_hbm.at[0], xext.at[pl.ds(PAD, rows)], load_sem)
    fetches = [
        pltpu.make_async_copy(source, target, table_sem.at[i])
        for i, (source, target) in enumerate((
            (piece_hbm, piece_ref), (ends_hbm, ends_ref), (first_hbm, first_ref), (second_hbm, second_ref),
            (kf_hbm, kf_ref), (off_hbm, off_ref), (compact_hbm, compact), (pooled_hbm, pooled_ref),
            (outer_hbm, outer_ref),
        ))
    ]
    reach = min(WIN, n) - 1
    middle = n // 2 - 1
    start = jnp.where(me >= n - 1, n - 1, jnp.where(me >= middle, middle, 0))
    stop = jnp.where(me < middle, middle, n - 1)
    first = jnp.maximum(jnp.minimum(start, me - 1), 0)
    last = jnp.minimum(jnp.maximum(stop - 1, me + 1), n - 1)
    near_first = first
    near_last = last
    far_first = jnp.minimum(jnp.maximum(me - reach, 0), near_first)
    far_last = jnp.where(me < middle, jnp.maximum(jnp.minimum(me + reach, n - 1), near_last), near_last)
    late_first = max(middle, n - 1 - reach)
    late_count = max(n - 2 - late_first, 0)
    late = (me >= late_first) & (me < n - 2)

    def greet(side, q, carry):
        pl.semaphore_signal(barrier, inc=1, device_id={"sec": q, "tile": side}, device_id_type=MESH)
        return carry

    lax.fori_loop(near_first, me, functools.partial(greet, 0), 0)
    lax.fori_loop(far_first, jnp.minimum(near_first, middle), functools.partial(greet, tiles - 1), 0)

    @pl.when(late)
    def _():
        greet(mt, n - 1, 0)

    far = far_last > near_last

    @pl.when(far & (mt > 0))
    def _():
        pl.semaphore_signal(barrier, inc=1, device_id={"tile": 0}, device_id_type=MESH)

    @pl.when(jnp.logical_not(far) & (mt == 0))
    def _():
        for side in range(1, tiles):
            pl.semaphore_signal(barrier, inc=1, device_id={"tile": side}, device_id_type=MESH)

    for fetch in fetches[:3]:
        fetch.start()
    load.start()
    for fetch in fetches[3:7]:
        fetch.start()

    for edge in (0, blocks + 1):
        at = slice(edge * LANES, (edge + 1) * LANES)
        vert[:, at] = jnp.zeros((rows, LANES), BF16)

    fetches[0].wait()
    fetches[1].wait()
    own = lax.broadcasted_iota(jnp.int32, (PATCH, LANES), 1) // KCOEF
    row_of = lax.broadcasted_iota(jnp.int32, (PATCH, LANES), 0)

    def build_columns(p, carry):
        at = pl.ds(pl.multiple_of(p * PATCH, PATCH), PATCH)
        for term in range(2):
            piece = piece_ref[term].astype(F32)
            ends = ends_ref[term].astype(F32)
            colw[term, at, 0:LANES] = jnp.where(own == p, piece[:, :LANES], 0.0).astype(BF16)
            slope = jnp.where(own == p, piece[:, LANES:], 0.0)
            slope = jnp.where((own == p + 1) & (row_of == PATCH - 1), ends[0:1], slope)
            slope = jnp.where((own == p - 1) & (row_of == 0), ends[1:2], slope)
            colw[term, at, LANES : 2 * LANES] = slope.astype(BF16)
        return carry

    lax.fori_loop(0, group // PATCH, build_columns, 0)
    side = lax.broadcasted_iota(jnp.int32, (LANES, LANES), 1) // KCOEF
    deep = lax.broadcasted_iota(jnp.int32, (LANES, LANES), 0)
    for term in range(2):
        ends = ends_ref[term].astype(F32)
        tail = jnp.where((side == LANES // KCOEF - 1) & (deep == 0), ends[1:2], 0.0)
        tail = jnp.where((side == 0) & (deep == LANES - 1), ends[0:1], tail)
        colw[term, group : group + LANES, 0:LANES] = jnp.zeros((LANES, LANES), BF16)
        colw[term, group : group + LANES, LANES : 2 * LANES] = tail.astype(BF16)

    fetches[2].wait()
    load.wait()
    for fetch in fetches[7:]:
        fetch.start()

    to_next = pltpu.make_async_remote_copy(
        src_ref=xext.at[pl.ds(rows, PAD)], dst_ref=xext.at[pl.ds(0, PAD)],
        send_sem=halo_ssem.at[0], recv_sem=halo_rsem.at[0],
        device_id={"tile": jnp.minimum(mt + 1, tiles - 1)}, device_id_type=MESH,
    )
    to_last = pltpu.make_async_remote_copy(
        src_ref=xext.at[pl.ds(PAD, PAD)], dst_ref=xext.at[pl.ds(PAD + rows, PAD)],
        send_sem=halo_ssem.at[1], recv_sem=halo_rsem.at[1],
        device_id={"tile": jnp.maximum(mt - 1, 0)}, device_id_type=MESH,
    )

    def send_halo():
        @pl.when(mt < tiles - 1)
        def _():
            to_next.start()

        @pl.when(mt > 0)
        def _():
            to_last.start()

    @pl.when(jnp.logical_not(far))
    def _():
        @pl.when(mt > 0)
        def _():
            pl.semaphore_wait(barrier, 1 + jnp.where(me == n - 1, late_count, 0))
            pl.semaphore_signal(pair_ok, inc=1, device_id={"tile": 0}, device_id_type=MESH)

        @pl.when(mt == 0)
        def _():
            pl.semaphore_wait(pair_ok, tiles - 1)

        send_halo()

    if late_count > 0:
        @pl.when(me == n - 1)
        def _():
            @pl.when(mt == 0)
            def _():
                pl.semaphore_wait(barrier, late_count)

            for q in range(late_first, n - 2):
                pl.semaphore_signal(late_ok, inc=1, device_id={"sec": q}, device_id_type=MESH)

    part = dot(first_ref[...], xext[PAD : PAD + rows, :])
    t_full = part[0:KCOEF] + part[KCOEF : 2 * KCOEF]
    lane8 = lax.broadcasted_iota(jnp.int32, (KCOEF, LANES), 1)
    edges = []
    for g in range(groups):
        edge = jnp.zeros((KCOEF, LANES), F32)
        if g > 0:
            edge = jnp.where(lane8 == LANES - 1, t_full[:, g * group - LANES : g * group], edge)
        if g < groups - 1:
            edge = jnp.where(lane8 == 0, t_full[:, (g + 1) * group : (g + 1) * group + LANES], edge)
        edges.append(edge)
    parts = split(jnp.concatenate([to_groups(t_full, group), jnp.concatenate(edges, axis=0)], axis=1), 2)
    size = groups * KCOEF
    wide = dot(jnp.concatenate(parts, axis=0), colw[0])
    wide = wide[:size] + wide[size:] + dot(parts[0], colw[1])
    desc = from_groups(wide[:, :LANES], groups).astype(BF16)
    dx = from_groups(wide[:, LANES:], groups)
    comm[me] = desc

    @pl.when(mt == 0)
    def _():
        count = tiles * (near_last - me) + jnp.where(far, tiles - 1, 0)

        @pl.when(count > 0)
        def _():
            pl.semaphore_wait(barrier, count)

        for side in range(1, tiles):
            pl.semaphore_signal(near_ok, inc=1, device_id={"tile": side}, device_id_type=MESH)

    @pl.when(mt > 0)
    def _():
        pl.semaphore_wait(near_ok, 1)


    def desc_copy(target):
        return pltpu.make_async_remote_copy(
            src_ref=comm.at[me], dst_ref=comm.at[me], send_sem=ssem.at[target], recv_sem=rsem.at[me],
            device_id={"sec": target}, device_id_type=MESH,
        )

    def send_desc(step, carry):
        desc_copy(me + 1 + step).start()
        return carry

    lax.fori_loop(0, last - me, send_desc, 0)

    pl.when(far)(send_halo)

    @pl.when(mt == 0)
    def _():
        xext[0:PAD, :] = jnp.zeros((PAD, cols), BF16)

    @pl.when(mt == tiles - 1)
    def _():
        xext[PAD + rows : 2 * PAD + rows, :] = jnp.zeros((PAD, cols), BF16)

    fetches[3].wait()

    @pl.when(mt < tiles - 1)
    def _():
        to_last.wait_recv()

    @pl.when(mt > 0)
    def _():
        to_next.wait_recv()

    part = dot(second_ref[...], xext[...])
    t_full = part[0:KCOEF] + part[KCOEF : 2 * KCOEF]
    for j in range(4):
        begin = 2 * KCOEF + j * sums
        sums_ref[j] = part[begin : begin + sums]
    for v in range(blocks):
        at = slice(v * LANES, (v + 1) * LANES)
        xtall[v] = xext[:, at].astype(F32)
    parts = split(to_groups(t_full, group), 2)
    wide = dot(jnp.concatenate(parts, axis=0), colw[0, 0:group, 0:LANES])
    dy = from_groups(wide[:size] + wide[size:] + dot(parts[0], colw[1, 0:group, 0:LANES]), groups)

    def row_total(value):
        for step in (4, 2, 1):
            value = value + pltpu.roll(value, step, 0)
        return value

    fetches[6].wait()

    def narrow(values):
        left = jnp.concatenate(values, axis=0)
        size = left.shape[0]
        wide = dot(jnp.concatenate(split(left, 3), axis=0), compact[...])
        total = wide[:size] + (wide[size : 2 * size] + wide[2 * size :])
        step = size // len(values)
        return [row_total(total[i * step : (i + 1) * step]) for i in range(len(values))]

    gxx, gxy, gyy = narrow([dx * dx, dx * dy, dy * dy])
    gxx = gxx + REG
    gyy = gyy + REG
    scale = 1.0 / (gxx * gyy - gxy * gxy)

    fetches[4].wait()
    fetches[5].wait()

    def wait_desc(q, carry):
        pltpu.make_async_remote_copy(
            src_ref=comm.at[q], dst_ref=comm.at[q], send_sem=ssem.at[q], recv_sem=rsem.at[q],
            device_id={"sec": q}, device_id_type=MESH,
        ).wait_recv()
        return carry

    lax.fori_loop(first, me, wait_desc, 0)

    keyref = comm[kf_ref[0]].astype(F32)
    predref = jnp.where(me > 0, comm[jnp.maximum(me - 1, 0)].astype(F32), 0.0)
    diff = 0.5 * (keyref + predref) - desc.astype(F32)
    bx, by = narrow([dx * diff, dy * diff])
    ux = (gyy * bx - gxy * by) * scale
    uy = (gxx * by - gxy * bx) * scale
    field_ref[0, 0] = ux[0:1, 0 : cols // PATCH]
    field_ref[0, 1] = uy[0:1, 0 : cols // PATCH]

    which = lax.broadcasted_iota(jnp.int32, (KCOEF, LANES), 0)
    second = which // 4
    source = jnp.where(lane8 < PATCH, 0, 1) + 2 * second

    def pick(shift):
        found = None
        for k, weight in enumerate(taps(shift)):
            found = weight if found is None else jnp.where(which - 4 * second == k, weight, found)
        return found

    def spread(kind, found):
        for i in range(blocks // 2):
            weights[kind, :, i * LANES : (i + 1) * LANES] = jnp.take_along_axis(found, source + 4 * i, axis=1)

    def combine(terms, kind, v):
        times = terms[0].shape[0] // KCOEF
        at = slice(v // 2 * LANES, (v // 2 + 1) * LANES)
        total = None
        for k, term in enumerate(terms):
            row = v % 2 * 4 + k
            term = stacked(jnp.broadcast_to(weights[kind, row : row + 1, at], (KCOEF, LANES)), times) * term
            total = term if total is None else total + term
        return total

    spread(1, pick(uy))
    picked_taps = pick(ux)
    none = jnp.zeros((sums, LANES), F32)
    totals = [none]
    for v in range(blocks):
        at = slice(v * LANES, (v + 1) * LANES)
        totals.append(combine([sums_ref[k, :, at] for k in range(4)], 1, v))
    totals.append(none)

    def turned(left, center, right, v):
        lane = lax.broadcasted_iota(jnp.int32, center.shape, 1)
        even = jnp.where(lane >= 96, left, center)
        odd = jnp.where(lane < 32, right, center)
        return (
            pltpu.roll(even, (LANES - off_ref[0, 2 * v]) & (LANES - 1), 1),
            pltpu.roll(odd, (LANES - off_ref[0, 2 * v + 1]) & (LANES - 1), 1),
        )

    rolled = [jnp.concatenate(turned(*totals[v : v + 3], v), axis=1) for v in range(blocks)]
    fetches[7].wait()
    slots = LANES // BOX
    per = LANES // slots
    slot = lane8 // slots
    for m in range(blocks // per):
        if m % 2 == 0:
            whole = dot(jnp.concatenate(rolled[m * per : (m + 2) * per], axis=0).astype(BF16), pooled_ref[...])
        wide = whole[m % 2 * per * sums : (m % 2 + 1) * per * sums]
        picked = None
        for i in range(per):
            piece = wide[i * sums : (i + 1) * sums]
            piece = [piece[:, j * LANES : (j + 1) * LANES] for j in range(4)]
            picked = piece if i == 0 else [jnp.where(slot == i, new, old) for new, old in zip(piece, picked)]
        at = slice(m * LANES, (m + 1) * LANES)
        small = jnp.take_along_axis(picked_taps, lane8 // BOX + m * slots, axis=1)
        total = None
        for k in range(4):
            term = jnp.broadcast_to(small[k : k + 1], (sums, LANES)) * picked[k]
            total = term if total is None else total + term
        block_ref[:, at] = total
        bsend[:, at] = total.astype(BF16)

    def block_copy(target):
        return pltpu.make_async_remote_copy(
            src_ref=bsend, dst_ref=brecv.at[target - me - 1], send_sem=bssem.at[target - me - 1],
            recv_sem=brsem.at[target - me - 1], device_id={"sec": target}, device_id_type=MESH,
        )

    def send_block(target, carry):
        block_copy(target).start()
        return carry

    nearest = jnp.minimum(near_last, me + reach)
    lax.fori_loop(0, nearest - me, lambda i, carry: send_block(nearest - i, carry), 0)

    @pl.when(late)
    def _():
        pl.semaphore_wait(late_ok, 1)
        send_block(n - 1, 0)

    @pl.when(far)
    def _():
        @pl.when(mt == tiles - 1)
        def _():
            pl.semaphore_wait(barrier, tiles * (far_last - near_last))
            for side in range(tiles - 1):
                pl.semaphore_signal(far_ok, inc=1, device_id={"tile": side}, device_id_type=MESH)

        @pl.when(mt < tiles - 1)
        def _():
            pl.semaphore_wait(far_ok, 1)

        lax.fori_loop(0, far_last - near_last, lambda i, carry: send_block(far_last - i, carry), 0)

    spread(0, picked_taps)
    fetches[8].wait()

    def vertical(v):
        total = combine([xtall[v, PAD + k : PAD + k + rows] for k in range(-1, 3)], 1, v)
        vert[:, (v + 1) * LANES : (v + 2) * LANES] = total.astype(BF16)

    def turn(v):
        even, odd = turned(*(vert[:, (v + i) * LANES : (v + i + 1) * LANES] for i in range(3)), v)
        lhs[v * rows : (v + 1) * rows, 0:LANES] = even
        lhs[v * rows : (v + 1) * rows, LANES : 2 * LANES] = odd

    lane64 = lax.broadcasted_iota(jnp.int32, (rows, LANES), 1)

    def across(g):
        wide = dot(lhs[g * CHUNK * rows : (g + 1) * CHUNK * rows, :], outer_ref[...])
        for i in range(CHUNK):
            v = g * CHUNK + i
            at = slice(v * LANES, (v + 1) * LANES)
            even = lhs[v * rows : (v + 1) * rows, 0:LANES]
            odd = lhs[v * rows : (v + 1) * rows, LANES : 2 * LANES]
            center = jnp.where(lane64 < PATCH, even, odd)
            after = pltpu.roll(jnp.where(((lane64 - 1) & (LANES - 1)) < PATCH, even, odd), LANES - 1, 1)
            piece = wide[i * rows : (i + 1) * rows]
            terms = [piece[:, :LANES], center.astype(F32), after.astype(F32), piece[:, LANES:]]
            obuf[0, :, at] = combine(terms, 0, v).astype(BF16)

    steps = blocks // CHUNK
    vertical(0)
    for step in range(steps + 2):
        if 0 <= step - 2:
            across(step - 2)
        if 0 <= step - 1 < steps:
            for i in range(CHUNK):
                turn((step - 1) * CHUNK + i)
        if step < steps:
            for i in range(CHUNK):
                if step * CHUNK + i + 1 < blocks:
                    vertical(step * CHUNK + i + 1)

    def sent_desc(target, carry):
        desc_copy(target).wait_send()
        return carry

    def sent_block(target, carry):
        block_copy(target).wait_send()
        return carry

    lax.fori_loop(me + 1, last + 1, sent_desc, 0)
    lax.fori_loop(me + 1, jnp.minimum(me + reach, n - 1) + 1, sent_block, 0)

    @pl.when(mt < tiles - 1)
    def _():
        to_next.wait_send()

    @pl.when(mt > 0)
    def _():
        to_last.wait_send()

    share = 1.0 / (BOX * BOX * WIN)
    pyr_ref[0] = block_ref[...] * share
    for d in range(reach, 0, -1):
        @pl.when(me >= d)
        def _():
            pltpu.make_async_remote_copy(
                src_ref=bsend, dst_ref=brecv.at[d - 1], send_sem=bssem.at[d - 1], recv_sem=brsem.at[d - 1],
                device_id={"sec": jnp.maximum(me - d, 0)}, device_id_type=MESH,
            ).wait_recv()
            pyr_ref[0] = pyr_ref[0] + brecv[d - 1].astype(F32) * share


def write_out(a, b, c, a_out, b_out, c_out, sem):
    copies = [
        pltpu.make_async_copy(source, target, sem.at[i])
        for i, (source, target) in enumerate(((a, a_out), (b, b_out), (c, c_out)))
    ]
    for copy in copies:
        copy.start()
    for copy in copies:
        copy.wait()


def body(n, tiles, image, keyframe, offsets):
    _, rows, cols = image.shape
    first, second = row_tables(rows)
    piece, ends = column_tables()
    outer, pooled = across_tables()
    ext = rows + 2 * PAD
    sums = rows // BOX
    coefs = cols // PATCH * KCOEF
    group = LANES // KCOEF * PATCH
    compact = gather_table(coefs)
    constants = (first, second, piece, ends, outer, pooled, compact)
    vmem = pl.BlockSpec(memory_space=pltpu.VMEM)
    hbm = pl.BlockSpec(memory_space=pltpu.HBM)
    dma = pltpu.SemaphoreType.DMA
    results = pl.pallas_call(
        functools.partial(kernel, n, tiles),
        out_shape=(
            pltpu.VMEM(image.shape, BF16),
            pltpu.VMEM((1, 2, 1, cols // PATCH), F32),
            pltpu.VMEM((1, sums, cols // BOX), F32),
        ),
        in_specs=[hbm] * (3 + len(constants)),
        out_specs=(vmem, vmem, vmem),
        scratch_shapes=[
            pltpu.SMEM((1,), jnp.int32),
            pltpu.SMEM((1, cols // PATCH), jnp.int32),
            *[pltpu.VMEM(value.shape, BF16) for value in constants],
            pltpu.VMEM((ext, cols), BF16),
            pltpu.VMEM((cols // LANES, ext, LANES), F32),
            pltpu.VMEM((2, group + LANES, 2 * LANES), BF16),
            pltpu.VMEM((n, KCOEF, coefs), BF16),
            pltpu.VMEM((4, sums, cols), F32),
            pltpu.VMEM((rows, cols + 2 * LANES), BF16),
            pltpu.VMEM((cols // LANES * rows, 2 * LANES), BF16),
            pltpu.VMEM((2, KCOEF, cols // 2), F32),
            pltpu.VMEM((WIN - 1, sums, cols // BOX), BF16),
            pltpu.VMEM((sums, cols // BOX), BF16),
            pltpu.VMEM((sums, cols // BOX), F32),
            dma,
            dma((9,)),
            dma((2,)),
            dma((2,)),
            dma((n,)),
            dma((n,)),
            dma((WIN - 1,)),
            dma((WIN - 1,)),
            *[pltpu.SemaphoreType.REGULAR] * 4,
        ],
        compiler_params=pltpu.CompilerParams(collective_id=0, has_side_effects=True),
    )(keyframe, offsets, *[jnp.asarray(value) for value in constants], image)
    return pl.pallas_call(
        write_out,
        out_shape=tuple(jax.ShapeDtypeStruct(r.shape, r.dtype) for r in results),
        in_specs=[vmem] * 3,
        out_specs=(hbm,) * 3,
        scratch_shapes=[dma((3,))],
    )(*[pltpu.with_memory_space_constraint(r, pltpu.VMEM) for r in results])


def solution(mesh):
    return jax.shard_map(
        functools.partial(body, mesh.shape["sec"], mesh.shape["tile"]),
        mesh=mesh,
        in_specs=(P(("slab", "sec"), "tile", None), P(("slab", "sec")), P(("slab", "sec"), None)),
        out_specs=(
            P(("slab", "sec"), "tile", None),
            P(("slab", "sec"), None, "tile", None),
            P(("slab", "sec"), "tile", None),
        ),
        check_vma=False,
    )
```

```python
import functools

import jax
import jax.numpy as jnp
import ml_dtypes
import numpy as np
from jax import lax
from jax.experimental import pallas as pl
from jax.experimental.pallas import tpu as pltpu
from jax.sharding import PartitionSpec as P

PATCH = 64
KCOEF = 8
WIN = 8
REG = 4.0
BOX = 8
LANES = 128
PAD = 16
CHUNK = 8
MESH = pl.DeviceIdType.MESH
F32 = jnp.float32
BF16 = jnp.bfloat16


def np_split(value, terms):
    parts = []
    rest = np.asarray(value, np.float64)
    for _ in range(terms):
        part = rest.astype(np.float32).astype(ml_dtypes.bfloat16)
        parts.append(part)
        rest = rest - part.astype(np.float64)
    return parts


def cosines():
    index = np.arange(PATCH, dtype=np.float64)
    order = np.arange(KCOEF, dtype=np.float64)
    table = np.sqrt(2.0 / PATCH) * np.cos(np.pi * (index[None, :] + 0.5) * order[:, None] / PATCH)
    table = table * np.where(order == 0, np.sqrt(0.5), 1.0)[:, None]
    return table.astype(np.float32).astype(np.float64)


def row_tables(rows):
    table = cosines()
    ext = rows + 2 * PAD
    first = np.concatenate(np_split(table, 2), axis=0)
    slope = np.zeros((KCOEF, ext))
    slope[:, PAD + 1 : PAD + 1 + rows] += 0.5 * table
    slope[:, PAD - 1 : PAD - 1 + rows] -= 0.5 * table
    second = np_split(slope, 2)
    for k in range(-1, 3):
        sums = np.zeros((rows // BOX, ext))
        for r in range(rows):
            sums[r // BOX, PAD + r + k] = 1.0
        second.append(sums.astype(ml_dtypes.bfloat16))
    return first, np.concatenate(second, axis=0)


def column_tables():
    table = cosines()
    slope = np.zeros((PATCH, KCOEF))
    slope[1:] += 0.5 * table.T[:-1]
    slope[:-1] -= 0.5 * table.T[1:]
    times = (1, LANES // KCOEF)
    pieces = []
    for both in (np_split(np.concatenate([np.tile(table.T, times), np.tile(slope, times)], axis=1), 2)):
        pieces.append(both)
    ends = np.zeros((16, LANES))
    ends[0] = np.tile(-0.5 * table[:, 0], LANES // KCOEF)
    ends[1] = np.tile(0.5 * table[:, PATCH - 1], LANES // KCOEF)
    return np.stack(pieces), np.stack(np_split(ends, 2))


def across_tables():
    shift = np.zeros((2 * LANES, 4, LANES))
    for k in range(-1, 3):
        for c in range(LANES):
            shift[(0 if c < PATCH else LANES) + (c + k) % LANES, k + 1, c] = 1.0
    slots = LANES // BOX
    pooled = shift.reshape(2 * LANES, 4, slots, BOX).sum(axis=3)
    pooled = np.tile(pooled, (1, 1, LANES // slots)).reshape(2 * LANES, 4 * LANES)
    outer = shift[:, (0, 3)].reshape(2 * LANES, 2 * LANES)
    return outer.astype(ml_dtypes.bfloat16), pooled.astype(ml_dtypes.bfloat16)


def gather_table(coefs):
    found = np.zeros((coefs, LANES))
    for i in range(coefs):
        found[i, i // KCOEF :: coefs // KCOEF] = 1.0
    return found.astype(ml_dtypes.bfloat16)


def split(value, terms):
    parts = []
    for _ in range(terms):
        part = value.astype(BF16)
        parts.append(part)
        value = value - part.astype(F32)
    return parts


def dot(a, b):
    return jnp.dot(a, b, preferred_element_type=F32)


def to_groups(value, width):
    count = value.shape[1] // width
    return jnp.concatenate([value[:, g * width : (g + 1) * width] for g in range(count)], axis=0)


def from_groups(value, count):
    rows = value.shape[0] // count
    return jnp.concatenate([value[g * rows : (g + 1) * rows] for g in range(count)], axis=1)


def taps(shift):
    return (
        -shift * (shift - 1.0) * (shift - 2.0) * (1.0 / 6.0),
        (shift + 1.0) * (shift - 1.0) * (shift - 2.0) * 0.5,
        -(shift + 1.0) * shift * (shift - 2.0) * 0.5,
        (shift + 1.0) * shift * (shift - 1.0) * (1.0 / 6.0),
    )


def stacked(value, times):
    return value if times == 1 else jnp.concatenate([value] * times, axis=0)


def kernel(
    n, tiles, kf_hbm, off_hbm, first_hbm, second_hbm, piece_hbm, ends_hbm, outer_hbm, pooled_hbm, compact_hbm, x_hbm,
    obuf, field_ref, block_ref, brecv,
    kf_ref, off_ref, first_ref, second_ref, piece_ref, ends_ref, outer_ref, pooled_ref, compact,
    xext, xtall, colw, comm, sums_ref, vert, lhs, weights, bsend,
    load_sem, table_sem, halo_ssem, halo_rsem, ssem, rsem, bssem, brsem, near_ok, far_ok, pair_ok, late_ok,
):
    me = lax.axis_index("sec")
    mt = lax.axis_index("tile")
    _, rows, cols = obuf.shape
    group = LANES // KCOEF * PATCH
    groups = cols // group
    blocks = cols // LANES
    sums = rows // BOX

    barrier = pltpu.get_barrier_semaphore()
    load = pltpu.make_async_copy(x_hbm.at[0], xext.at[pl.ds(PAD, rows)], load_sem)
    fetches = [
        pltpu.make_async_copy(source, target, table_sem.at[i])
        for i, (source, target) in enumerate((
            (piece_hbm, piece_ref), (ends_hbm, ends_ref), (first_hbm, first_ref), (second_hbm, second_ref),
            (kf_hbm, kf_ref), (off_hbm, off_ref), (compact_hbm, compact), (pooled_hbm, pooled_ref),
            (outer_hbm, outer_ref),
        ))
    ]
    reach = min(WIN, n) - 1
    middle = n // 2 - 1
    start = jnp.where(me >= n - 1, n - 1, jnp.where(me >= middle, middle, 0))
    stop = jnp.where(me < middle, middle, n - 1)
    first = jnp.maximum(jnp.minimum(start, me - 1), 0)
    last = jnp.minimum(jnp.maximum(stop - 1, me + 1), n - 1)
    near_first = first
    near_last = last
    far_first = jnp.minimum(jnp.maximum(me - reach, 0), near_first)
    far_last = jnp.where(me < middle, jnp.maximum(jnp.minimum(me + reach, n - 1), near_last), near_last)
    late_first = max(middle, n - 1 - reach)
    late_count = max(n - 2 - late_first, 0)
    late = (me >= late_first) & (me < n - 2)

    def greet(side, q, carry):
        pl.semaphore_signal(barrier, inc=1, device_id={"sec": q, "tile": side}, device_id_type=MESH)
        return carry

    lax.fori_loop(near_first, me, functools.partial(greet, 0), 0)
    lax.fori_loop(far_first, jnp.minimum(near_first, middle), functools.partial(greet, tiles - 1), 0)

    @pl.when(late)
    def _():
        greet(mt, n - 1, 0)

    far = far_last > near_last

    @pl.when(far & (mt > 0))
    def _():
        pl.semaphore_signal(barrier, inc=1, device_id={"tile": 0}, device_id_type=MESH)

    @pl.when(jnp.logical_not(far) & (mt == 0))
    def _():
        for side in range(1, tiles):
            pl.semaphore_signal(barrier, inc=1, device_id={"tile": side}, device_id_type=MESH)

    for fetch in fetches[:3]:
        fetch.start()
    load.start()
    for fetch in fetches[3:7]:
        fetch.start()

    for edge in (0, blocks + 1):
        at = slice(edge * LANES, (edge + 1) * LANES)
        vert[:, at] = jnp.zeros((rows, LANES), BF16)

    for d in range(1, brecv.shape[0] + 1):
        @pl.when(me < d)
        def _():
            brecv[d - 1] = jnp.zeros(brecv.shape[1:], BF16)

    fetches[0].wait()
    fetches[1].wait()
    own = lax.broadcasted_iota(jnp.int32, (PATCH, LANES), 1) // KCOEF
    row_of = lax.broadcasted_iota(jnp.int32, (PATCH, LANES), 0)

    def build_columns(p, carry):
        at = pl.ds(pl.multiple_of(p * PATCH, PATCH), PATCH)
        for term in range(2):
            piece = piece_ref[term].astype(F32)
            ends = ends_ref[term].astype(F32)
            colw[term, at, 0:LANES] = jnp.where(own == p, piece[:, :LANES], 0.0).astype(BF16)
            slope = jnp.where(own == p, piece[:, LANES:], 0.0)
            slope = jnp.where((own == p + 1) & (row_of == PATCH - 1), ends[0:1], slope)
            slope = jnp.where((own == p - 1) & (row_of == 0), ends[1:2], slope)
            colw[term, at, LANES : 2 * LANES] = slope.astype(BF16)
        return carry

    lax.fori_loop(0, group // PATCH, build_columns, 0)
    side = lax.broadcasted_iota(jnp.int32, (LANES, LANES), 1) // KCOEF
    deep = lax.broadcasted_iota(jnp.int32, (LANES, LANES), 0)
    for term in range(2):
        ends = ends_ref[term].astype(F32)
        tail = jnp.where((side == LANES // KCOEF - 1) & (deep == 0), ends[1:2], 0.0)
        tail = jnp.where((side == 0) & (deep == LANES - 1), ends[0:1], tail)
        colw[term, group : group + LANES, 0:LANES] = jnp.zeros((LANES, LANES), BF16)
        colw[term, group : group + LANES, LANES : 2 * LANES] = tail.astype(BF16)

    fetches[2].wait()
    load.wait()
    for fetch in fetches[7:]:
        fetch.start()

    to_next = pltpu.make_async_remote_copy(
        src_ref=xext.at[pl.ds(rows, PAD)], dst_ref=xext.at[pl.ds(0, PAD)],
        send_sem=halo_ssem.at[0], recv_sem=halo_rsem.at[0],
        device_id={"tile": jnp.minimum(mt + 1, tiles - 1)}, device_id_type=MESH,
    )
    to_last = pltpu.make_async_remote_copy(
        src_ref=xext.at[pl.ds(PAD, PAD)], dst_ref=xext.at[pl.ds(PAD + rows, PAD)],
        send_sem=halo_ssem.at[1], recv_sem=halo_rsem.at[1],
        device_id={"tile": jnp.maximum(mt - 1, 0)}, device_id_type=MESH,
    )

    def send_halo():
        @pl.when(mt < tiles - 1)
        def _():
            to_next.start()

        @pl.when(mt > 0)
        def _():
            to_last.start()

    @pl.when(jnp.logical_not(far))
    def _():
        @pl.when(mt > 0)
        def _():
            pl.semaphore_wait(barrier, 1 + jnp.where(me == n - 1, late_count, 0))
            pl.semaphore_signal(pair_ok, inc=1, device_id={"tile": 0}, device_id_type=MESH)

        @pl.when(mt == 0)
        def _():
            pl.semaphore_wait(pair_ok, tiles - 1)

        send_halo()

    if late_count > 0:
        @pl.when(me == n - 1)
        def _():
            @pl.when(mt == 0)
            def _():
                pl.semaphore_wait(barrier, late_count)

            for q in range(late_first, n - 2):
                pl.semaphore_signal(late_ok, inc=1, device_id={"sec": q}, device_id_type=MESH)

    part = dot(first_ref[...], xext[PAD : PAD + rows, :])
    t_full = part[0:KCOEF] + part[KCOEF : 2 * KCOEF]
    lane8 = lax.broadcasted_iota(jnp.int32, (KCOEF, LANES), 1)
    edges = []
    for g in range(groups):
        edge = jnp.zeros((KCOEF, LANES), F32)
        if g > 0:
            edge = jnp.where(lane8 == LANES - 1, t_full[:, g * group - LANES : g * group], edge)
        if g < groups - 1:
            edge = jnp.where(lane8 == 0, t_full[:, (g + 1) * group : (g + 1) * group + LANES], edge)
        edges.append(edge)
    parts = split(jnp.concatenate([to_groups(t_full, group), jnp.concatenate(edges, axis=0)], axis=1), 2)
    size = groups * KCOEF
    wide = dot(jnp.concatenate(parts, axis=0), colw[0])
    wide = wide[:size] + wide[size:] + dot(parts[0], colw[1])
    desc = from_groups(wide[:, :LANES], groups).astype(BF16)
    dx = from_groups(wide[:, LANES:], groups)
    comm[me] = desc

    @pl.when(mt == 0)
    def _():
        count = tiles * (near_last - me) + jnp.where(far, tiles - 1, 0)

        @pl.when(count > 0)
        def _():
            pl.semaphore_wait(barrier, count)

        for side in range(1, tiles):
            pl.semaphore_signal(near_ok, inc=1, device_id={"tile": side}, device_id_type=MESH)

    @pl.when(mt > 0)
    def _():
        pl.semaphore_wait(near_ok, 1)


    def desc_copy(target):
        return pltpu.make_async_remote_copy(
            src_ref=comm.at[me], dst_ref=comm.at[me], send_sem=ssem.at[target], recv_sem=rsem.at[me],
            device_id={"sec": target}, device_id_type=MESH,
        )

    def send_desc(step, carry):
        desc_copy(me + 1 + step).start()
        return carry

    lax.fori_loop(0, last - me, send_desc, 0)

    pl.when(far)(send_halo)

    @pl.when(mt == 0)
    def _():
        xext[0:PAD, :] = jnp.zeros((PAD, cols), BF16)

    @pl.when(mt == tiles - 1)
    def _():
        xext[PAD + rows : 2 * PAD + rows, :] = jnp.zeros((PAD, cols), BF16)

    fetches[3].wait()

    @pl.when(mt < tiles - 1)
    def _():
        to_last.wait_recv()

    @pl.when(mt > 0)
    def _():
        to_next.wait_recv()

    part = dot(second_ref[...], xext[...])
    t_full = part[0:KCOEF] + part[KCOEF : 2 * KCOEF]
    for j in range(4):
        begin = 2 * KCOEF + j * sums
        sums_ref[j] = part[begin : begin + sums]
    for v in range(blocks):
        at = slice(v * LANES, (v + 1) * LANES)
        xtall[v] = xext[:, at].astype(F32)
    parts = split(to_groups(t_full, group), 2)
    wide = dot(jnp.concatenate(parts, axis=0), colw[0, 0:group, 0:LANES])
    dy = from_groups(wide[:size] + wide[size:] + dot(parts[0], colw[1, 0:group, 0:LANES]), groups)

    def row_total(value):
        for step in (4, 2, 1):
            value = value + pltpu.roll(value, step, 0)
        return value

    fetches[6].wait()

    def narrow(values):
        left = jnp.concatenate(values, axis=0)
        size = left.shape[0]
        wide = dot(jnp.concatenate(split(left, 3), axis=0), compact[...])
        total = wide[:size] + (wide[size : 2 * size] + wide[2 * size :])
        step = size // len(values)
        return [row_total(total[i * step : (i + 1) * step]) for i in range(len(values))]

    gxx, gxy, gyy = narrow([dx * dx, dx * dy, dy * dy])
    gxx = gxx + REG
    gyy = gyy + REG
    scale = 1.0 / (gxx * gyy - gxy * gxy)

    fetches[4].wait()
    fetches[5].wait()

    def wait_desc(q, carry):
        pltpu.make_async_remote_copy(
            src_ref=comm.at[q], dst_ref=comm.at[q], send_sem=ssem.at[q], recv_sem=rsem.at[q],
            device_id={"sec": q}, device_id_type=MESH,
        ).wait_recv()
        return carry

    lax.fori_loop(first, me, wait_desc, 0)

    keyref = comm[kf_ref[0]].astype(F32)
    predref = jnp.where(me > 0, comm[jnp.maximum(me - 1, 0)].astype(F32), 0.0)
    diff = 0.5 * (keyref + predref) - desc.astype(F32)
    bx, by = narrow([dx * diff, dy * diff])
    ux = (gyy * bx - gxy * by) * scale
    uy = (gxx * by - gxy * bx) * scale
    field_ref[0, 0] = ux[0:1, 0 : cols // PATCH]
    field_ref[0, 1] = uy[0:1, 0 : cols // PATCH]

    which = lax.broadcasted_iota(jnp.int32, (KCOEF, LANES), 0)
    second = which // 4
    source = jnp.where(lane8 < PATCH, 0, 1) + 2 * second

    def pick(shift):
        found = None
        for k, weight in enumerate(taps(shift)):
            found = weight if found is None else jnp.where(which - 4 * second == k, weight, found)
        return found

    def spread(kind, found):
        for i in range(blocks // 2):
            weights[kind, :, i * LANES : (i + 1) * LANES] = jnp.take_along_axis(found, source + 4 * i, axis=1)

    def combine(terms, kind, v):
        times = terms[0].shape[0] // KCOEF
        at = slice(v // 2 * LANES, (v // 2 + 1) * LANES)
        total = None
        for k, term in enumerate(terms):
            row = v % 2 * 4 + k
            term = stacked(jnp.broadcast_to(weights[kind, row : row + 1, at], (KCOEF, LANES)), times) * term
            total = term if total is None else total + term
        return total

    spread(1, pick(uy))
    picked_taps = pick(ux)
    none = jnp.zeros((sums, LANES), F32)
    totals = [none]
    for v in range(blocks):
        at = slice(v * LANES, (v + 1) * LANES)
        totals.append(combine([sums_ref[k, :, at] for k in range(4)], 1, v))
    totals.append(none)

    def turned(left, center, right, v):
        lane = lax.broadcasted_iota(jnp.int32, center.shape, 1)
        even = jnp.where(lane >= 96, left, center)
        odd = jnp.where(lane < 32, right, center)
        return (
            pltpu.roll(even, (LANES - off_ref[0, 2 * v]) & (LANES - 1), 1),
            pltpu.roll(odd, (LANES - off_ref[0, 2 * v + 1]) & (LANES - 1), 1),
        )

    rolled = [jnp.concatenate(turned(*totals[v : v + 3], v), axis=1) for v in range(blocks)]
    fetches[7].wait()
    slots = LANES // BOX
    per = LANES // slots
    slot = lane8 // slots
    for m in range(blocks // per):
        if m % 2 == 0:
            whole = dot(jnp.concatenate(rolled[m * per : (m + 2) * per], axis=0).astype(BF16), pooled_ref[...])
        wide = whole[m % 2 * per * sums : (m % 2 + 1) * per * sums]
        picked = None
        for i in range(per):
            piece = wide[i * sums : (i + 1) * sums]
            piece = [piece[:, j * LANES : (j + 1) * LANES] for j in range(4)]
            picked = piece if i == 0 else [jnp.where(slot == i, new, old) for new, old in zip(piece, picked)]
        at = slice(m * LANES, (m + 1) * LANES)
        small = jnp.take_along_axis(picked_taps, lane8 // BOX + m * slots, axis=1)
        total = None
        for k in range(4):
            term = jnp.broadcast_to(small[k : k + 1], (sums, LANES)) * picked[k]
            total = term if total is None else total + term
        block_ref[:, at] = total
        bsend[:, at] = total.astype(BF16)

    def block_copy(target):
        return pltpu.make_async_remote_copy(
            src_ref=bsend, dst_ref=brecv.at[target - me - 1], send_sem=bssem.at[target - me - 1],
            recv_sem=brsem.at[target - me - 1], device_id={"sec": target}, device_id_type=MESH,
        )

    def send_block(target, carry):
        block_copy(target).start()
        return carry

    nearest = jnp.minimum(near_last, me + reach)
    lax.fori_loop(0, nearest - me, lambda i, carry: send_block(nearest - i, carry), 0)

    @pl.when(late)
    def _():
        pl.semaphore_wait(late_ok, 1)
        send_block(n - 1, 0)

    @pl.when(far)
    def _():
        @pl.when(mt == tiles - 1)
        def _():
            pl.semaphore_wait(barrier, tiles * (far_last - near_last))
            for side in range(tiles - 1):
                pl.semaphore_signal(far_ok, inc=1, device_id={"tile": side}, device_id_type=MESH)

        @pl.when(mt < tiles - 1)
        def _():
            pl.semaphore_wait(far_ok, 1)

        lax.fori_loop(0, far_last - near_last, lambda i, carry: send_block(far_last - i, carry), 0)

    spread(0, picked_taps)
    fetches[8].wait()

    def vertical(v):
        total = combine([xtall[v, PAD + k : PAD + k + rows] for k in range(-1, 3)], 1, v)
        vert[:, (v + 1) * LANES : (v + 2) * LANES] = total.astype(BF16)

    def turn(v):
        even, odd = turned(*(vert[:, (v + i) * LANES : (v + i + 1) * LANES] for i in range(3)), v)
        lhs[v * rows : (v + 1) * rows, 0:LANES] = even
        lhs[v * rows : (v + 1) * rows, LANES : 2 * LANES] = odd

    lane64 = lax.broadcasted_iota(jnp.int32, (rows, LANES), 1)

    def across(g):
        wide = dot(lhs[g * CHUNK * rows : (g + 1) * CHUNK * rows, :], outer_ref[...])
        for i in range(CHUNK):
            v = g * CHUNK + i
            at = slice(v * LANES, (v + 1) * LANES)
            even = lhs[v * rows : (v + 1) * rows, 0:LANES]
            odd = lhs[v * rows : (v + 1) * rows, LANES : 2 * LANES]
            center = jnp.where(lane64 < PATCH, even, odd)
            after = pltpu.roll(jnp.where(((lane64 - 1) & (LANES - 1)) < PATCH, even, odd), LANES - 1, 1)
            piece = wide[i * rows : (i + 1) * rows]
            terms = [piece[:, :LANES], center.astype(F32), after.astype(F32), piece[:, LANES:]]
            obuf[0, :, at] = combine(terms, 0, v).astype(BF16)

    steps = blocks // CHUNK
    vertical(0)
    for step in range(steps + 2):
        if 0 <= step - 2:
            across(step - 2)
        if 0 <= step - 1 < steps:
            for i in range(CHUNK):
                turn((step - 1) * CHUNK + i)
        if step < steps:
            for i in range(CHUNK):
                if step * CHUNK + i + 1 < blocks:
                    vertical(step * CHUNK + i + 1)

    def sent_desc(target, carry):
        desc_copy(target).wait_send()
        return carry

    def sent_block(target, carry):
        block_copy(target).wait_send()
        return carry

    lax.fori_loop(me + 1, last + 1, sent_desc, 0)
    lax.fori_loop(me + 1, jnp.minimum(me + reach, n - 1) + 1, sent_block, 0)

    @pl.when(mt < tiles - 1)
    def _():
        to_next.wait_send()

    @pl.when(mt > 0)
    def _():
        to_last.wait_send()

    for d in range(reach, 0, -1):
        @pl.when(me >= d)
        def _():
            pltpu.make_async_remote_copy(
                src_ref=bsend, dst_ref=brecv.at[d - 1], send_sem=bssem.at[d - 1], recv_sem=brsem.at[d - 1],
                device_id={"sec": jnp.maximum(me - d, 0)}, device_id_type=MESH,
            ).wait_recv()


def write_out(a, b, block, others, a_out, b_out, c_out, c, sem):
    copies = [
        pltpu.make_async_copy(source, target, sem.at[i])
        for i, (source, target) in enumerate(((a, a_out), (b, b_out), (c, c_out)))
    ]
    copies[0].start()
    copies[1].start()
    total = block[...]
    for d in range(others.shape[0]):
        total = total + others[d].astype(F32)
    c[0] = total * (1.0 / (BOX * BOX * WIN))
    copies[2].start()
    for copy in copies:
        copy.wait()


def body(n, tiles, image, keyframe, offsets):
    _, rows, cols = image.shape
    first, second = row_tables(rows)
    piece, ends = column_tables()
    outer, pooled = across_tables()
    ext = rows + 2 * PAD
    sums = rows // BOX
    coefs = cols // PATCH * KCOEF
    group = LANES // KCOEF * PATCH
    compact = gather_table(coefs)
    constants = (first, second, piece, ends, outer, pooled, compact)
    vmem = pl.BlockSpec(memory_space=pltpu.VMEM)
    hbm = pl.BlockSpec(memory_space=pltpu.HBM)
    dma = pltpu.SemaphoreType.DMA
    results = pl.pallas_call(
        functools.partial(kernel, n, tiles),
        out_shape=(
            pltpu.VMEM(image.shape, BF16),
            pltpu.VMEM((1, 2, 1, cols // PATCH), F32),
            pltpu.VMEM((sums, cols // BOX), F32),
            pltpu.VMEM((WIN - 1, sums, cols // BOX), BF16),
        ),
        in_specs=[hbm] * (3 + len(constants)),
        out_specs=(vmem,) * 4,
        scratch_shapes=[
            pltpu.SMEM((1,), jnp.int32),
            pltpu.SMEM((1, cols // PATCH), jnp.int32),
            *[pltpu.VMEM(value.shape, BF16) for value in constants],
            pltpu.VMEM((ext, cols), BF16),
            pltpu.VMEM((cols // LANES, ext, LANES), F32),
            pltpu.VMEM((2, group + LANES, 2 * LANES), BF16),
            pltpu.VMEM((n, KCOEF, coefs), BF16),
            pltpu.VMEM((4, sums, cols), F32),
            pltpu.VMEM((rows, cols + 2 * LANES), BF16),
            pltpu.VMEM((cols // LANES * rows, 2 * LANES), BF16),
            pltpu.VMEM((2, KCOEF, cols // 2), F32),
            pltpu.VMEM((sums, cols // BOX), BF16),
            dma,
            dma((9,)),
            dma((2,)),
            dma((2,)),
            dma((n,)),
            dma((n,)),
            dma((WIN - 1,)),
            dma((WIN - 1,)),
            *[pltpu.SemaphoreType.REGULAR] * 4,
        ],
        compiler_params=pltpu.CompilerParams(collective_id=0, has_side_effects=True),
    )(keyframe, offsets, *[jnp.asarray(value) for value in constants], image)
    return pl.pallas_call(
        write_out,
        out_shape=(
            *(jax.ShapeDtypeStruct(r.shape, r.dtype) for r in results[:2]),
            jax.ShapeDtypeStruct((1, sums, cols // BOX), F32),
        ),
        in_specs=[vmem] * 4,
        out_specs=(hbm,) * 3,
        scratch_shapes=[pltpu.VMEM((1, sums, cols // BOX), F32), dma((3,))],
    )(*[pltpu.with_memory_space_constraint(r, pltpu.VMEM) for r in results])


def solution(mesh):
    return jax.shard_map(
        functools.partial(body, mesh.shape["sec"], mesh.shape["tile"]),
        mesh=mesh,
        in_specs=(P(("slab", "sec"), "tile", None), P(("slab", "sec")), P(("slab", "sec"), None)),
        out_specs=(
            P(("slab", "sec"), "tile", None),
            P(("slab", "sec"), None, "tile", None),
            P(("slab", "sec"), "tile", None),
        ),
        check_vma=False,
    )
```

```python
import functools

import jax
import jax.numpy as jnp
import ml_dtypes
import numpy as np
from jax import lax
from jax.experimental import pallas as pl
from jax.experimental.pallas import tpu as pltpu
from jax.sharding import PartitionSpec as P

PATCH = 64
KCOEF = 8
WIN = 8
REG = 4.0
BOX = 8
LANES = 128
PAD = 16
CHUNK = 8
MESH = pl.DeviceIdType.MESH
F32 = jnp.float32
BF16 = jnp.bfloat16


def np_split(value, terms):
    parts = []
    rest = np.asarray(value, np.float64)
    for _ in range(terms):
        part = rest.astype(np.float32).astype(ml_dtypes.bfloat16)
        parts.append(part)
        rest = rest - part.astype(np.float64)
    return parts


def cosines():
    index = np.arange(PATCH, dtype=np.float64)
    order = np.arange(KCOEF, dtype=np.float64)
    table = np.sqrt(2.0 / PATCH) * np.cos(np.pi * (index[None, :] + 0.5) * order[:, None] / PATCH)
    table = table * np.where(order == 0, np.sqrt(0.5), 1.0)[:, None]
    return table.astype(np.float32).astype(np.float64)


def row_tables(rows):
    table = cosines()
    ext = rows + 2 * PAD
    first = np.concatenate(np_split(table, 2), axis=0)
    slope = np.zeros((KCOEF, ext))
    slope[:, PAD + 1 : PAD + 1 + rows] += 0.5 * table
    slope[:, PAD - 1 : PAD - 1 + rows] -= 0.5 * table
    second = np_split(slope, 2)
    for k in range(-1, 3):
        sums = np.zeros((rows // BOX, ext))
        for r in range(rows):
            sums[r // BOX, PAD + r + k] = 1.0
        second.append(sums.astype(ml_dtypes.bfloat16))
    return first, np.concatenate(second, axis=0)


def column_tables():
    table = cosines()
    slope = np.zeros((PATCH, KCOEF))
    slope[1:] += 0.5 * table.T[:-1]
    slope[:-1] -= 0.5 * table.T[1:]
    times = (1, LANES // KCOEF)
    pieces = []
    for both in (np_split(np.concatenate([np.tile(table.T, times), np.tile(slope, times)], axis=1), 2)):
        pieces.append(both)
    ends = np.zeros((16, LANES))
    ends[0] = np.tile(-0.5 * table[:, 0], LANES // KCOEF)
    ends[1] = np.tile(0.5 * table[:, PATCH - 1], LANES // KCOEF)
    return np.stack(pieces), np.stack(np_split(ends, 2))


def across_tables():
    shift = np.zeros((2 * LANES, 4, LANES))
    for k in range(-1, 3):
        for c in range(LANES):
            shift[(0 if c < PATCH else LANES) + (c + k) % LANES, k + 1, c] = 1.0
    slots = LANES // BOX
    pooled = shift.reshape(2 * LANES, 4, slots, BOX).sum(axis=3)
    pooled = np.tile(pooled, (1, 1, LANES // slots)).reshape(2 * LANES, 4 * LANES)
    outer = shift[:, (0, 3)].reshape(2 * LANES, 2 * LANES)
    return outer.astype(ml_dtypes.bfloat16), pooled.astype(ml_dtypes.bfloat16)


def gather_table(coefs):
    found = np.zeros((coefs, LANES))
    for i in range(coefs):
        found[i, i // KCOEF :: coefs // KCOEF] = 1.0
    return found.astype(ml_dtypes.bfloat16)


def split(value, terms):
    parts = []
    for _ in range(terms):
        part = value.astype(BF16)
        parts.append(part)
        value = value - part.astype(F32)
    return parts


def dot(a, b):
    return jnp.dot(a, b, preferred_element_type=F32)


def to_groups(value, width):
    count = value.shape[1] // width
    return jnp.concatenate([value[:, g * width : (g + 1) * width] for g in range(count)], axis=0)


def from_groups(value, count):
    rows = value.shape[0] // count
    return jnp.concatenate([value[g * rows : (g + 1) * rows] for g in range(count)], axis=1)


def taps(shift):
    return (
        -shift * (shift - 1.0) * (shift - 2.0) * (1.0 / 6.0),
        (shift + 1.0) * (shift - 1.0) * (shift - 2.0) * 0.5,
        -(shift + 1.0) * shift * (shift - 2.0) * 0.5,
        (shift + 1.0) * shift * (shift - 1.0) * (1.0 / 6.0),
    )


def stacked(value, times):
    return value if times == 1 else jnp.concatenate([value] * times, axis=0)


def kernel(
    n, tiles, kf_hbm, off_hbm, first_hbm, second_hbm, piece_hbm, ends_hbm, outer_hbm, pooled_hbm, compact_hbm, x_hbm,
    obuf, field_ref, block_ref, brecv,
    kf_ref, off_ref, first_ref, second_ref, piece_ref, ends_ref, outer_ref, pooled_ref, compact,
    xext, xtall, colw, comm, sums_ref, vert, lhs, weights, bsend,
    load_sem, table_sem, halo_ssem, halo_rsem, ssem, rsem, bssem, brsem, near_ok, far_ok, pair_ok, late_ok,
):
    me = lax.axis_index("sec")
    mt = lax.axis_index("tile")
    _, rows, cols = obuf.shape
    group = LANES // KCOEF * PATCH
    groups = cols // group
    blocks = cols // LANES
    sums = rows // BOX

    barrier = pltpu.get_barrier_semaphore()
    load = pltpu.make_async_copy(x_hbm.at[0], xext.at[pl.ds(PAD, rows)], load_sem)
    fetches = [
        pltpu.make_async_copy(source, target, table_sem.at[i])
        for i, (source, target) in enumerate((
            (piece_hbm, piece_ref), (ends_hbm, ends_ref), (first_hbm, first_ref), (second_hbm, second_ref),
            (kf_hbm, kf_ref), (off_hbm, off_ref), (compact_hbm, compact), (pooled_hbm, pooled_ref),
            (outer_hbm, outer_ref),
        ))
    ]
    reach = min(WIN, n) - 1
    middle = n // 2 - 1
    start = jnp.where(me >= n - 1, n - 1, jnp.where(me >= middle, middle, 0))
    stop = jnp.where(me < middle, middle, n - 1)
    first = jnp.maximum(jnp.minimum(start, me - 1), 0)
    last = jnp.minimum(jnp.maximum(stop - 1, me + 1), n - 1)
    near_first = first
    near_last = last
    far_first = jnp.minimum(jnp.maximum(me - reach, 0), near_first)
    far_last = jnp.where(me < middle, jnp.maximum(jnp.minimum(me + reach, n - 1), near_last), near_last)
    late_first = max(middle, n - 1 - reach)
    late_count = max(n - 2 - late_first, 0)
    late = (me >= late_first) & (me < n - 2)

    def greet(side, q, carry):
        pl.semaphore_signal(barrier, inc=1, device_id={"sec": q, "tile": side}, device_id_type=MESH)
        return carry

    lax.fori_loop(near_first, me, functools.partial(greet, 0), 0)
    lax.fori_loop(far_first, jnp.minimum(near_first, middle), functools.partial(greet, tiles - 1), 0)

    @pl.when(late)
    def _():
        greet(mt, n - 1, 0)

    far = far_last > near_last

    @pl.when(far & (mt > 0))
    def _():
        pl.semaphore_signal(barrier, inc=1, device_id={"tile": 0}, device_id_type=MESH)

    @pl.when(jnp.logical_not(far) & (mt == 0))
    def _():
        for side in range(1, tiles):
            pl.semaphore_signal(barrier, inc=1, device_id={"tile": side}, device_id_type=MESH)

    for fetch in fetches[:3]:
        fetch.start()
    load.start()
    for fetch in fetches[3:7]:
        fetch.start()

    for edge in (0, blocks + 1):
        at = slice(edge * LANES, (edge + 1) * LANES)
        vert[:, at] = jnp.zeros((rows, LANES), BF16)

    for d in range(1, brecv.shape[0] + 1):
        @pl.when(me < d)
        def _():
            brecv[d - 1] = jnp.zeros(brecv.shape[1:], BF16)

    fetches[0].wait()
    fetches[1].wait()
    own = lax.broadcasted_iota(jnp.int32, (PATCH, LANES), 1) // KCOEF
    row_of = lax.broadcasted_iota(jnp.int32, (PATCH, LANES), 0)

    def build_columns(p, carry):
        at = pl.ds(pl.multiple_of(p * PATCH, PATCH), PATCH)
        for term in range(2):
            piece = piece_ref[term].astype(F32)
            ends = ends_ref[term].astype(F32)
            colw[term, at, 0:LANES] = jnp.where(own == p, piece[:, :LANES], 0.0).astype(BF16)
            slope = jnp.where(own == p, piece[:, LANES:], 0.0)
            slope = jnp.where((own == p + 1) & (row_of == PATCH - 1), ends[0:1], slope)
            slope = jnp.where((own == p - 1) & (row_of == 0), ends[1:2], slope)
            colw[term, at, LANES : 2 * LANES] = slope.astype(BF16)
        return carry

    lax.fori_loop(0, group // PATCH, build_columns, 0)
    side = lax.broadcasted_iota(jnp.int32, (LANES, LANES), 1) // KCOEF
    deep = lax.broadcasted_iota(jnp.int32, (LANES, LANES), 0)
    for term in range(2):
        ends = ends_ref[term].astype(F32)
        tail = jnp.where((side == LANES // KCOEF - 1) & (deep == 0), ends[1:2], 0.0)
        tail = jnp.where((side == 0) & (deep == LANES - 1), ends[0:1], tail)
        colw[term, group : group + LANES, 0:LANES] = jnp.zeros((LANES, LANES), BF16)
        colw[term, group : group + LANES, LANES : 2 * LANES] = tail.astype(BF16)

    fetches[2].wait()
    load.wait()
    for fetch in fetches[7:]:
        fetch.start()

    to_next = pltpu.make_async_remote_copy(
        src_ref=xext.at[pl.ds(rows, PAD)], dst_ref=xext.at[pl.ds(0, PAD)],
        send_sem=halo_ssem.at[0], recv_sem=halo_rsem.at[0],
        device_id={"tile": jnp.minimum(mt + 1, tiles - 1)}, device_id_type=MESH,
    )
    to_last = pltpu.make_async_remote_copy(
        src_ref=xext.at[pl.ds(PAD, PAD)], dst_ref=xext.at[pl.ds(PAD + rows, PAD)],
        send_sem=halo_ssem.at[1], recv_sem=halo_rsem.at[1],
        device_id={"tile": jnp.maximum(mt - 1, 0)}, device_id_type=MESH,
    )

    def send_halo():
        @pl.when(mt < tiles - 1)
        def _():
            to_next.start()

        @pl.when(mt > 0)
        def _():
            to_last.start()

    @pl.when(jnp.logical_not(far))
    def _():
        @pl.when(mt > 0)
        def _():
            pl.semaphore_wait(barrier, 1 + jnp.where(me == n - 1, late_count, 0))
            pl.semaphore_signal(pair_ok, inc=1, device_id={"tile": 0}, device_id_type=MESH)

        @pl.when(mt == 0)
        def _():
            pl.semaphore_wait(pair_ok, tiles - 1)

        send_halo()

    if late_count > 0:
        @pl.when(me == n - 1)
        def _():
            @pl.when(mt == 0)
            def _():
                pl.semaphore_wait(barrier, late_count)

            for q in range(late_first, n - 2):
                pl.semaphore_signal(late_ok, inc=1, device_id={"sec": q}, device_id_type=MESH)

    part = dot(first_ref[...], xext[PAD : PAD + rows, :])
    t_full = part[0:KCOEF] + part[KCOEF : 2 * KCOEF]
    lane8 = lax.broadcasted_iota(jnp.int32, (KCOEF, LANES), 1)
    edges = []
    for g in range(groups):
        edge = jnp.zeros((KCOEF, LANES), F32)
        if g > 0:
            edge = jnp.where(lane8 == LANES - 1, t_full[:, g * group - LANES : g * group], edge)
        if g < groups - 1:
            edge = jnp.where(lane8 == 0, t_full[:, (g + 1) * group : (g + 1) * group + LANES], edge)
        edges.append(edge)
    parts = split(jnp.concatenate([to_groups(t_full, group), jnp.concatenate(edges, axis=0)], axis=1), 2)
    size = groups * KCOEF
    wide = dot(jnp.concatenate(parts, axis=0), colw[0])
    wide = wide[:size] + wide[size:] + dot(parts[0], colw[1])
    desc = from_groups(wide[:, :LANES], groups).astype(BF16)
    dx = from_groups(wide[:, LANES:], groups)
    comm[me] = desc

    @pl.when(mt == 0)
    def _():
        count = tiles * (near_last - me) + jnp.where(far, tiles - 1, 0)

        @pl.when(count > 0)
        def _():
            pl.semaphore_wait(barrier, count)

        for side in range(1, tiles):
            pl.semaphore_signal(near_ok, inc=1, device_id={"tile": side}, device_id_type=MESH)

    @pl.when(mt > 0)
    def _():
        pl.semaphore_wait(near_ok, 1)


    def desc_copy(target):
        return pltpu.make_async_remote_copy(
            src_ref=comm.at[me], dst_ref=comm.at[me], send_sem=ssem.at[target], recv_sem=rsem.at[me],
            device_id={"sec": target}, device_id_type=MESH,
        )

    def send_desc(step, carry):
        desc_copy(me + 1 + step).start()
        return carry

    lax.fori_loop(0, last - me, send_desc, 0)

    pl.when(far)(send_halo)

    @pl.when(mt == 0)
    def _():
        xext[0:PAD, :] = jnp.zeros((PAD, cols), BF16)

    @pl.when(mt == tiles - 1)
    def _():
        xext[PAD + rows : 2 * PAD + rows, :] = jnp.zeros((PAD, cols), BF16)

    fetches[3].wait()

    @pl.when(mt < tiles - 1)
    def _():
        to_last.wait_recv()

    @pl.when(mt > 0)
    def _():
        to_next.wait_recv()

    part = dot(second_ref[...], xext[...])
    t_full = part[0:KCOEF] + part[KCOEF : 2 * KCOEF]
    for j in range(4):
        begin = 2 * KCOEF + j * sums
        sums_ref[j] = part[begin : begin + sums]
    for v in range(blocks):
        at = slice(v * LANES, (v + 1) * LANES)
        xtall[v] = xext[:, at].astype(F32)
    parts = split(to_groups(t_full, group), 2)
    wide = dot(jnp.concatenate(parts, axis=0), colw[0, 0:group, 0:LANES])
    dy = from_groups(wide[:size] + wide[size:] + dot(parts[0], colw[1, 0:group, 0:LANES]), groups)

    def row_total(value):
        for step in (4, 2, 1):
            value = value + pltpu.roll(value, step, 0)
        return value

    fetches[6].wait()

    def narrow(values):
        left = jnp.concatenate(values, axis=0)
        size = left.shape[0]
        wide = dot(jnp.concatenate(split(left, 3), axis=0), compact[...])
        total = wide[:size] + (wide[size : 2 * size] + wide[2 * size :])
        step = size // len(values)
        return [row_total(total[i * step : (i + 1) * step]) for i in range(len(values))]

    gxx, gxy, gyy = narrow([dx * dx, dx * dy, dy * dy])
    gxx = gxx + REG
    gyy = gyy + REG
    scale = 1.0 / (gxx * gyy - gxy * gxy)

    fetches[4].wait()
    fetches[5].wait()

    def wait_desc(q, carry):
        pltpu.make_async_remote_copy(
            src_ref=comm.at[q], dst_ref=comm.at[q], send_sem=ssem.at[q], recv_sem=rsem.at[q],
            device_id={"sec": q}, device_id_type=MESH,
        ).wait_recv()
        return carry

    lax.fori_loop(first, me, wait_desc, 0)

    keyref = comm[kf_ref[0]].astype(F32)
    predref = jnp.where(me > 0, comm[jnp.maximum(me - 1, 0)].astype(F32), 0.0)
    diff = 0.5 * (keyref + predref) - desc.astype(F32)
    bx, by = narrow([dx * diff, dy * diff])
    ux = (gyy * bx - gxy * by) * scale
    uy = (gxx * by - gxy * bx) * scale
    field_ref[0, 0] = ux[0:1, 0 : cols // PATCH]
    field_ref[0, 1] = uy[0:1, 0 : cols // PATCH]

    which = lax.broadcasted_iota(jnp.int32, (KCOEF, LANES), 0)
    second = which // 4
    source = jnp.where(lane8 < PATCH, 0, 1) + 2 * second

    def pick(shift):
        found = None
        for k, weight in enumerate(taps(shift)):
            found = weight if found is None else jnp.where(which - 4 * second == k, weight, found)
        return found

    def spread(kind, found):
        for i in range(blocks // 2):
            weights[kind, :, i * LANES : (i + 1) * LANES] = jnp.take_along_axis(found, source + 4 * i, axis=1)

    def combine(terms, kind, v):
        times = terms[0].shape[0] // KCOEF
        at = slice(v // 2 * LANES, (v // 2 + 1) * LANES)
        total = None
        for k, term in enumerate(terms):
            row = v % 2 * 4 + k
            term = stacked(jnp.broadcast_to(weights[kind, row : row + 1, at], (KCOEF, LANES)), times) * term
            total = term if total is None else total + term
        return total

    spread(1, pick(uy))
    picked_taps = pick(ux)
    none = jnp.zeros((sums, LANES), F32)
    totals = [none]
    for v in range(blocks):
        at = slice(v * LANES, (v + 1) * LANES)
        totals.append(combine([sums_ref[k, :, at] for k in range(4)], 1, v))
    totals.append(none)

    def turned(left, center, right, v):
        lane = lax.broadcasted_iota(jnp.int32, center.shape, 1)
        even = jnp.where(lane >= 96, left, center)
        odd = jnp.where(lane < 32, right, center)
        return (
            pltpu.roll(even, (LANES - off_ref[0, 2 * v]) & (LANES - 1), 1),
            pltpu.roll(odd, (LANES - off_ref[0, 2 * v + 1]) & (LANES - 1), 1),
        )

    rolled = [jnp.concatenate(turned(*totals[v : v + 3], v), axis=1) for v in range(blocks)]
    fetches[7].wait()
    slots = LANES // BOX
    per = LANES // slots
    slot = lane8 // slots
    for m in range(blocks // per):
        if m % 2 == 0:
            whole = dot(jnp.concatenate(rolled[m * per : (m + 2) * per], axis=0).astype(BF16), pooled_ref[...])
        wide = whole[m % 2 * per * sums : (m % 2 + 1) * per * sums]
        picked = None
        for i in range(per):
            piece = wide[i * sums : (i + 1) * sums]
            piece = [piece[:, j * LANES : (j + 1) * LANES] for j in range(4)]
            picked = piece if i == 0 else [jnp.where(slot == i, new, old) for new, old in zip(piece, picked)]
        at = slice(m * LANES, (m + 1) * LANES)
        small = jnp.take_along_axis(picked_taps, lane8 // BOX + m * slots, axis=1)
        total = None
        for k in range(4):
            term = jnp.broadcast_to(small[k : k + 1], (sums, LANES)) * picked[k]
            total = term if total is None else total + term
        block_ref[:, at] = total
        bsend[:, at] = total.astype(BF16)

    def block_copy(target):
        return pltpu.make_async_remote_copy(
            src_ref=bsend, dst_ref=brecv.at[target - me - 1], send_sem=bssem.at[target - me - 1],
            recv_sem=brsem.at[target - me - 1], device_id={"sec": target}, device_id_type=MESH,
        )

    def send_block(target, carry):
        block_copy(target).start()
        return carry

    nearest = jnp.minimum(near_last, me + reach)
    lax.fori_loop(0, nearest - me, lambda i, carry: send_block(me + 1 + i, carry), 0)

    @pl.when(late)
    def _():
        pl.semaphore_wait(late_ok, 1)
        send_block(n - 1, 0)

    @pl.when(far)
    def _():
        @pl.when(mt == tiles - 1)
        def _():
            pl.semaphore_wait(barrier, tiles * (far_last - near_last))
            for side in range(tiles - 1):
                pl.semaphore_signal(far_ok, inc=1, device_id={"tile": side}, device_id_type=MESH)

        @pl.when(mt < tiles - 1)
        def _():
            pl.semaphore_wait(far_ok, 1)

        lax.fori_loop(0, far_last - near_last, lambda i, carry: send_block(far_last - i, carry), 0)

    spread(0, picked_taps)
    fetches[8].wait()

    def vertical(v):
        total = combine([xtall[v, PAD + k : PAD + k + rows] for k in range(-1, 3)], 1, v)
        vert[:, (v + 1) * LANES : (v + 2) * LANES] = total.astype(BF16)

    def turn(v):
        even, odd = turned(*(vert[:, (v + i) * LANES : (v + i + 1) * LANES] for i in range(3)), v)
        lhs[v * rows : (v + 1) * rows, 0:LANES] = even
        lhs[v * rows : (v + 1) * rows, LANES : 2 * LANES] = odd

    lane64 = lax.broadcasted_iota(jnp.int32, (rows, LANES), 1)

    def across(g):
        wide = dot(lhs[g * CHUNK * rows : (g + 1) * CHUNK * rows, :], outer_ref[...])
        for i in range(CHUNK):
            v = g * CHUNK + i
            at = slice(v * LANES, (v + 1) * LANES)
            even = lhs[v * rows : (v + 1) * rows, 0:LANES]
            odd = lhs[v * rows : (v + 1) * rows, LANES : 2 * LANES]
            center = jnp.where(lane64 < PATCH, even, odd)
            after = pltpu.roll(jnp.where(((lane64 - 1) & (LANES - 1)) < PATCH, even, odd), LANES - 1, 1)
            piece = wide[i * rows : (i + 1) * rows]
            terms = [piece[:, :LANES], center.astype(F32), after.astype(F32), piece[:, LANES:]]
            obuf[0, :, at] = combine(terms, 0, v).astype(BF16)

    steps = blocks // CHUNK
    vertical(0)
    for step in range(steps + 2):
        if 0 <= step - 2:
            across(step - 2)
        if 0 <= step - 1 < steps:
            for i in range(CHUNK):
                turn((step - 1) * CHUNK + i)
        if step < steps:
            for i in range(CHUNK):
                if step * CHUNK + i + 1 < blocks:
                    vertical(step * CHUNK + i + 1)

    def sent_desc(target, carry):
        desc_copy(target).wait_send()
        return carry

    def sent_block(target, carry):
        block_copy(target).wait_send()
        return carry

    lax.fori_loop(me + 1, last + 1, sent_desc, 0)
    lax.fori_loop(me + 1, jnp.minimum(me + reach, n - 1) + 1, sent_block, 0)

    @pl.when(mt < tiles - 1)
    def _():
        to_next.wait_send()

    @pl.when(mt > 0)
    def _():
        to_last.wait_send()

    for d in range(reach, 0, -1):
        @pl.when(me >= d)
        def _():
            pltpu.make_async_remote_copy(
                src_ref=bsend, dst_ref=brecv.at[d - 1], send_sem=bssem.at[d - 1], recv_sem=brsem.at[d - 1],
                device_id={"sec": jnp.maximum(me - d, 0)}, device_id_type=MESH,
            ).wait_recv()


def write_out(a, b, block, others, a_out, b_out, c_out, c, sem):
    copies = [
        pltpu.make_async_copy(source, target, sem.at[i])
        for i, (source, target) in enumerate(((a, a_out), (b, b_out), (c, c_out)))
    ]
    copies[0].start()
    copies[1].start()
    total = block[...]
    for d in range(others.shape[0]):
        total = total + others[d].astype(F32)
    c[0] = total * (1.0 / (BOX * BOX * WIN))
    copies[2].start()
    for copy in copies:
        copy.wait()


def body(n, tiles, image, keyframe, offsets):
    _, rows, cols = image.shape
    first, second = row_tables(rows)
    piece, ends = column_tables()
    outer, pooled = across_tables()
    ext = rows + 2 * PAD
    sums = rows // BOX
    coefs = cols // PATCH * KCOEF
    group = LANES // KCOEF * PATCH
    compact = gather_table(coefs)
    constants = (first, second, piece, ends, outer, pooled, compact)
    vmem = pl.BlockSpec(memory_space=pltpu.VMEM)
    hbm = pl.BlockSpec(memory_space=pltpu.HBM)
    dma = pltpu.SemaphoreType.DMA
    results = pl.pallas_call(
        functools.partial(kernel, n, tiles),
        out_shape=(
            pltpu.VMEM(image.shape, BF16),
            pltpu.VMEM((1, 2, 1, cols // PATCH), F32),
            pltpu.VMEM((sums, cols // BOX), F32),
            pltpu.VMEM((WIN - 1, sums, cols // BOX), BF16),
        ),
        in_specs=[hbm] * (3 + len(constants)),
        out_specs=(vmem,) * 4,
        scratch_shapes=[
            pltpu.SMEM((1,), jnp.int32),
            pltpu.SMEM((1, cols // PATCH), jnp.int32),
            *[pltpu.VMEM(value.shape, BF16) for value in constants],
            pltpu.VMEM((ext, cols), BF16),
            pltpu.VMEM((cols // LANES, ext, LANES), F32),
            pltpu.VMEM((2, group + LANES, 2 * LANES), BF16),
            pltpu.VMEM((n, KCOEF, coefs), BF16),
            pltpu.VMEM((4, sums, cols), F32),
            pltpu.VMEM((rows, cols + 2 * LANES), BF16),
            pltpu.VMEM((cols // LANES * rows, 2 * LANES), BF16),
            pltpu.VMEM((2, KCOEF, cols // 2), F32),
            pltpu.VMEM((sums, cols // BOX), BF16),
            dma,
            dma((9,)),
            dma((2,)),
            dma((2,)),
            dma((n,)),
            dma((n,)),
            dma((WIN - 1,)),
            dma((WIN - 1,)),
            *[pltpu.SemaphoreType.REGULAR] * 4,
        ],
        compiler_params=pltpu.CompilerParams(collective_id=0, has_side_effects=True),
    )(keyframe, offsets, *[jnp.asarray(value) for value in constants], image)
    return pl.pallas_call(
        write_out,
        out_shape=(
            *(jax.ShapeDtypeStruct(r.shape, r.dtype) for r in results[:2]),
            jax.ShapeDtypeStruct((1, sums, cols // BOX), F32),
        ),
        in_specs=[vmem] * 4,
        out_specs=(hbm,) * 3,
        scratch_shapes=[pltpu.VMEM((1, sums, cols // BOX), F32), dma((3,))],
    )(*[pltpu.with_memory_space_constraint(r, pltpu.VMEM) for r in results])


def solution(mesh):
    return jax.shard_map(
        functools.partial(body, mesh.shape["sec"], mesh.shape["tile"]),
        mesh=mesh,
        in_specs=(P(("slab", "sec"), "tile", None), P(("slab", "sec")), P(("slab", "sec"), None)),
        out_specs=(
            P(("slab", "sec"), "tile", None),
            P(("slab", "sec"), None, "tile", None),
            P(("slab", "sec"), "tile", None),
        ),
        check_vma=False,
    )
```
